256 devices in a mesh: ctx: 32 (over y, x, core), head: 8 (over z).
Axes of the slice: x: 4, y: 4, z: 8, core: 2. Of those that a mesh axis runs over, the one named last changes fastest.
Arguments:
- queries: bfloat16 [8192, 4096], P('ctx', 'head'), may hold values from -168 to 168, as said below
- keys: bfloat16 [8192, 1024], P('ctx', 'head'), may hold values from -6.05 to 6.05, as said below
- values: bfloat16 [8192, 1024], P('ctx', 'head'), may hold values from -6 to 6
- d_y: bfloat16 [8192, 4096], P('ctx', 'head'), may hold values from -6 to 6
- w_out: bfloat16 [4096, 4096], P('head'), may hold values from -0.09375 to 0.09375
- key_blocks: int32 [64, 32], replicated, may hold values from 0 to 63, as said below
- block_count: int32 [64], replicated, may hold values from 1 to 32, as said below
Outputs:
- d_queries: bfloat16 [8192, 4096], P('ctx', 'head')
- keys_gradient: bfloat16 [8192, 1024], P('ctx', 'head')
- values_gradient: bfloat16 [8192, 1024], P('ctx', 'head')
The draws below stay inside these ranges and needn't reach their ends.
Inputs may be any that keep to these rules, and one draw needn't show every extreme that they name: `key_blocks`: each row holds 32 distinct block numbers; its first block_count entries are at most the query block's own number, and the first entry is that number. Later entries are read by nobody. `block_count`: the last query block has 32 live entries; query block b has at most b // 2 + 1. `queries`: values stay within the bound. `keys`: values stay within the bound.
All inputs are finite; a program needn't handle non-finite values.
Results may differ from the reference program's by a relative error of at most 0.017.
Values may be sent and summed in bfloat16 or wider, within the bound.
No kernel may reach another device: no remote copies, remote signals or barrier semaphores. Data moves between devices by JAX's collectives and lax.ppermute only.
A program may use at most 64 MiB of HBM per device.

```python
import jax
import jax.numpy as jnp
from jax import lax

D = 4096
HQ = 32
SHARED_KV_SLOTS = 8
FEATURE_WIDTH = 128
QUERY_GROUP = 4
SPAN_LENGTH = 128
TOKEN_COUNT = 8192
QUERY_BLOCKS = 64
VISIBLE_SPANS = 32


def unshaped_keys(key):
    return jax.random.truncated_normal(jax.random.fold_in(key, 11), -6.0, 6.0, (TOKEN_COUNT, SHARED_KV_SLOTS * FEATURE_WIDTH), jnp.float32)


def draw_keys(key, part):
    base_offset = unshaped_keys(key)
    return base_offset.astype(jnp.bfloat16)


def draw_queries(key, part):
    base_offset = jax.random.truncated_normal(jax.random.fold_in(key, 12), -6.0, 6.0, (TOKEN_COUNT, HQ * FEATURE_WIDTH), jnp.float32)
    return base_offset.astype(jnp.bfloat16)


def mask_tables(key):
    block_indices = jnp.arange(QUERY_BLOCKS, dtype=jnp.int32)
    low = block_indices // 4
    high = block_indices // 2 + 1
    counts = jax.random.randint(jax.random.fold_in(key, 21), (QUERY_BLOCKS,), low, high) + 1
    counts = jnp.where(block_indices == QUERY_BLOCKS - 1, VISIBLE_SPANS, counts).astype(jnp.int32)
    starts = jax.random.randint(jax.random.fold_in(key, 22), (QUERY_BLOCKS,), 0, 4) == 0
    turn_ids = jnp.cumsum(starts.astype(jnp.int32))
    rows = block_indices[:, None]
    cols = block_indices[None, :]
    earlier = cols < rows
    same_turn = turn_ids[None, :] == turn_ids[:, None]
    priority = jnp.where(cols == rows, 4, jnp.where(earlier & (cols == 0), 3, jnp.where(earlier & same_turn, 2, jnp.where(earlier, 1, 0))))
    noise = jax.random.randint(jax.random.fold_in(key, 23), (QUERY_BLOCKS, QUERY_BLOCKS), 0, 4096)
    ranking = priority * 2 ** 24 + noise * QUERY_BLOCKS + cols
    _, chosen = jax.lax.top_k(ranking.astype(jnp.int32), VISIBLE_SPANS)
    return (chosen.astype(jnp.int32), counts)


def draw_key_blocks(key, part):
    return mask_tables(key)[0]


def draw_block_count(key, part):
    return mask_tables(key)[1]


def block_scale(own_key, shape, shards, low, largest):
    gain, own = 1.0, jax.random.fold_in(own_key, 6)
    for dim, parts in shards:
        draws = jnp.exp(jax.random.uniform(jax.random.fold_in(own, dim), (parts,), jnp.float32, low / len(shards), largest / len(shards)))
        gain = gain * jnp.repeat(draws, shape[dim] // parts).reshape([-1 if axis == dim else 1 for axis in range(len(shape))])
    return gain


def gaussian(key, dims, deviation, reach, pieces=(), held_as=jnp.bfloat16):
    drawn = deviation * jax.random.normal(key, dims, jnp.float32)
    if pieces:
        drawn = drawn * block_scale(key, dims, pieces, -0.22, 0.18)
    return jnp.clip(drawn, -reach, reach).astype(held_as)


def setup_inputs(seed: int = 0) -> dict:
    splits = jax.random.split(jax.random.key(seed), 8)
    return {
        "queries": draw_queries(jax.random.fold_in(splits[7], 71), 0),
        "keys": draw_keys(jax.random.fold_in(splits[7], 71), 0),
        "values": gaussian(splits[2], (TOKEN_COUNT, SHARED_KV_SLOTS * FEATURE_WIDTH), 1.0, 6.0, ((0, 32), (1, 8))),
        "d_y": gaussian(splits[3], (TOKEN_COUNT, D), 1.0, 6.0, ((0, 32), (1, 8))),
        "w_out": gaussian(splits[4], (HQ * FEATURE_WIDTH, D), (HQ * FEATURE_WIDTH) ** -0.5, 0.09375, ((0, 8),)),
        "key_blocks": draw_key_blocks(jax.random.fold_in(splits[7], 71), 0),
        "block_count": draw_block_count(jax.random.fold_in(splits[7], 71), 0),
    }


def block_grads(query_block_rows, gradient_rows, key_everything, value_everything, key_blocks, block_count, query_blk):
    score_scale = 1.0 / (FEATURE_WIDTH ** 0.5)
    block_indices = key_blocks[query_blk]
    key_selected = key_everything.reshape(QUERY_BLOCKS, SPAN_LENGTH, SHARED_KV_SLOTS, FEATURE_WIDTH)[block_indices].reshape(VISIBLE_SPANS * SPAN_LENGTH, SHARED_KV_SLOTS, FEATURE_WIDTH).astype(jnp.float32)
    value_selected = value_everything.reshape(QUERY_BLOCKS, SPAN_LENGTH, SHARED_KV_SLOTS, FEATURE_WIDTH)[block_indices].reshape(VISIBLE_SPANS * SPAN_LENGTH, SHARED_KV_SLOTS, FEATURE_WIDTH).astype(jnp.float32)
    asker_vectors_wide = query_block_rows.reshape(SPAN_LENGTH, SHARED_KV_SLOTS, QUERY_GROUP, FEATURE_WIDTH).astype(jnp.float32)
    upstream_derivative_wide = gradient_rows.reshape(SPAN_LENGTH, SHARED_KV_SLOTS, QUERY_GROUP, FEATURE_WIDTH).astype(jnp.float32)
    slot_live = jnp.arange(VISIBLE_SPANS, dtype=jnp.int32) < block_count[query_blk]
    key_pos = (block_indices[:, None] * SPAN_LENGTH + jnp.arange(SPAN_LENGTH, dtype=jnp.int32)[None, :]).reshape(VISIBLE_SPANS * SPAN_LENGTH)
    key_live = jnp.repeat(slot_live, SPAN_LENGTH)
    query_pos = query_blk * SPAN_LENGTH + jnp.arange(SPAN_LENGTH, dtype=jnp.int32)
    allowed = key_live[None, :] & (key_pos[None, :] <= query_pos[:, None])
    scores = jnp.einsum('ihgd,jhd->hgij', asker_vectors_wide, key_selected) * score_scale
    scores = jnp.where(allowed, scores, -jnp.inf)
    row_max = jnp.max(scores, axis=-1, keepdims=True)
    log_total = row_max + jnp.log(jnp.sum(jnp.exp(scores - row_max), axis=-1, keepdims=True))
    probs = jnp.where(allowed, jnp.exp(scores - log_total), 0.0)
    d_probs = jnp.einsum('ihgd,jhd->hgij', upstream_derivative_wide, value_selected)
    row_delta = jnp.sum(probs * d_probs, axis=-1, keepdims=True)
    logit_derivative = lax.optimization_barrier((probs * (d_probs - row_delta) * score_scale).astype(jnp.bfloat16)).astype(jnp.float32)
    attention_weights_narrow = lax.optimization_barrier(probs.astype(jnp.bfloat16)).astype(jnp.float32)
    d_query = jnp.einsum('hgij,jhd->ihgd', logit_derivative, key_selected).reshape(SPAN_LENGTH, HQ * FEATURE_WIDTH)
    lookup_derivative = jnp.einsum('ftbu,bfth->ufh', logit_derivative, asker_vectors_wide).reshape(VISIBLE_SPANS, SPAN_LENGTH, SHARED_KV_SLOTS * FEATURE_WIDTH)
    payload_derivative = jnp.einsum('ftbu,bfth->ufh', attention_weights_narrow, upstream_derivative_wide).reshape(VISIBLE_SPANS, SPAN_LENGTH, SHARED_KV_SLOTS * FEATURE_WIDTH)
    return d_query.astype(jnp.bfloat16), lookup_derivative, payload_derivative, block_indices


def reference(queries, keys, values, d_y, w_out, key_blocks, block_count):
    att_grad = jnp.dot(d_y, w_out.T, preferred_element_type=jnp.float32).astype(jnp.bfloat16)

    def step(carried, query_blk):
        key_gradient_total, value_gradient_total = carried
        query_block_rows = lax.dynamic_slice_in_dim(queries, query_blk * SPAN_LENGTH, SPAN_LENGTH, 0)
        gradient_rows = lax.dynamic_slice_in_dim(att_grad, query_blk * SPAN_LENGTH, SPAN_LENGTH, 0)
        d_query, lookup_derivative, payload_derivative, block_indices = block_grads(query_block_rows, gradient_rows, keys, values, key_blocks, block_count, query_blk)
        key_gradient_total = key_gradient_total.at[block_indices].add(lookup_derivative)
        value_gradient_total = value_gradient_total.at[block_indices].add(payload_derivative)
        return (key_gradient_total, value_gradient_total), d_query

    zeroed_totals = jnp.zeros((QUERY_BLOCKS, SPAN_LENGTH, SHARED_KV_SLOTS * FEATURE_WIDTH), jnp.float32)
    (key_gradient_total, value_gradient_total), d_queries = lax.scan(step, (zeroed_totals, zeroed_totals), jnp.arange(QUERY_BLOCKS, dtype=jnp.int32))
    d_queries = d_queries.reshape(TOKEN_COUNT, HQ * FEATURE_WIDTH)
    keys_gradient = key_gradient_total.reshape(TOKEN_COUNT, SHARED_KV_SLOTS * FEATURE_WIDTH).astype(jnp.bfloat16)
    values_gradient = value_gradient_total.reshape(TOKEN_COUNT, SHARED_KV_SLOTS * FEATURE_WIDTH).astype(jnp.bfloat16)
    return (d_queries, keys_gradient, values_gradient)
```

```python
import functools
import math

import jax
import jax.numpy as jnp
from jax import lax
from jax.experimental import pallas as pl
from jax.experimental.pallas import tpu as pltpu
from jax.sharding import Mesh
from jax.sharding import PartitionSpec as P

WIDTH = 128
SPAN = 128
HEADS = 4
ROWS = HEADS * SPAN
SCALE = 1.0 / math.sqrt(WIDTH)
LOG2E = 1.4426950408889634
NEG = -1e30
TILE = 2
CHIP_AXES = ("y", "x")
NT = (((1,), (1,)), ((), ()))
TN = (((0,), (0,)), ((), ()))
f32 = jnp.float32
bf16 = jnp.bfloat16


def my_chip():
    return lax.axis_index("y") * lax.axis_size("x") + lax.axis_index("x")


def query_block(j, chip, core):
    side = jnp.where(j < 2, core, 1 - core)
    return 4 * chip + 2 * side + j % 2


def stack_heads(dst, own, sib):
    for j in range(4):
        src = own if j < 2 else sib
        for h in range(HEADS):
            dst[j, h * SPAN : (h + 1) * SPAN, :] = src[
                (j % 2) * SPAN : (j % 2 + 1) * SPAN, h * WIDTH : (h + 1) * WIDTH
            ]


def list_blocks(kb, bc, lst, b, core):
    def step(s, n):
        blk = kb[b, s]
        lst[n] = 2 * (blk // 4) + blk % 2
        return n + jnp.where((blk // 2) % 2 == core, 1, 0)

    return lax.fori_loop(1, bc[b], step, 0)


def rows_of(ref, idxs, lo):
    parts = [
        ref[pl.ds(pl.multiple_of(i * SPAN, SPAN), SPAN), lo : lo + WIDTH] for i in idxs
    ]
    return parts[0] if len(parts) == 1 else jnp.concatenate(parts, axis=0)


def causal_mask():
    key = lax.broadcasted_iota(jnp.int32, (SPAN, ROWS), 0)
    qry = lax.broadcasted_iota(jnp.int32, (SPAN, ROWS), 1) % SPAN
    return key <= qry


def walk(kb, bc, lst, b, chip, core, visit, carry):
    n = list_blocks(kb, bc, lst, b, core)
    own_diag = (b // 2) % 2 == core
    diag = 2 * (b // 4) + b % 2
    carry = lax.cond(own_diag, lambda c: visit(c, [diag], True), lambda c: c, carry)
    tiles = n // TILE
    carry = lax.fori_loop(
        0, tiles, lambda t, c: visit(c, [lst[t * TILE + i] for i in range(TILE)], False), carry
    )
    return lax.fori_loop(tiles * TILE, n, lambda t, c: visit(c, [lst[t]], False), carry)


def forward_kernel(kb, bc, q_own, q_sib, kv, out, qs, acc, lst):
    chip, core = my_chip(), lax.axis_index("core")
    stack_heads(qs, q_own, q_sib)

    def per_block(j, _):
        b = query_block(j, chip, core)
        acc[...] = jnp.zeros_like(acc)

        def visit(carry, idxs, masked):
            m, l = carry
            k = rows_of(kv, idxs, 0)
            v = rows_of(kv, idxs, WIDTH)
            s = lax.dot_general(k, qs[j], NT, preferred_element_type=f32) * (SCALE * LOG2E)
            if masked:
                s = jnp.where(causal_mask(), s, NEG)
            m_new = jnp.maximum(m, jnp.max(s, axis=0, keepdims=True))
            alpha = jnp.exp2(m - m_new)
            p = jnp.exp2(s - m_new)
            hi = p.astype(bf16)
            lo = (p - hi.astype(f32)).astype(bf16)
            o = lax.dot_general(v, hi, TN, preferred_element_type=f32)
            o += lax.dot_general(v, lo, TN, preferred_element_type=f32)
            acc[...] = acc[...] * alpha + o
            return m_new, l * alpha + jnp.sum(p, axis=0, keepdims=True)

        start = (jnp.full((1, ROWS), NEG, f32), jnp.zeros((1, ROWS), f32))
        m, l = walk(kb, bc, lst, b, chip, core, visit, start)
        out[j, :WIDTH, :] = acc[...]
        out[j, WIDTH : WIDTH + 8, :] = jnp.concatenate(
            [m, l, jnp.zeros((6, ROWS), f32)], axis=0
        )
        return 0

    lax.fori_loop(0, 4, per_block, 0)


def backward_kernel(
    kb, bc, q_own, q_sib, g_own, g_sib, kv, st_own, st_sib, dq_own, dq_sib, dkv, qs, gs, dq, acc, lst
):
    chip, core = my_chip(), lax.axis_index("core")
    stack_heads(qs, q_own, q_sib)
    stack_heads(gs, g_own, g_sib)
    acc[...] = jnp.zeros_like(acc)

    def per_block(j, _):
        b = query_block(j, chip, core)
        peer = (j + 2) % 4
        m0, l0 = st_own[j, WIDTH : WIDTH + 1, :], st_own[j, WIDTH + 1 : WIDTH + 2, :]
        m1, l1 = st_sib[peer, WIDTH : WIDTH + 1, :], st_sib[peer, WIDTH + 1 : WIDTH + 2, :]
        m = jnp.maximum(m0, m1)
        a0, a1 = jnp.exp2(m0 - m), jnp.exp2(m1 - m)
        l = l0 * a0 + l1 * a1
        total = m + jnp.log(l) * LOG2E
        o = st_own[j, :WIDTH, :] * (a0 / l) + st_sib[peer, :WIDTH, :] * (a1 / l)
        delta = jnp.concatenate(
            [
                jnp.sum(
                    o[:, h * SPAN : (h + 1) * SPAN]
                    * gs[j, h * SPAN : (h + 1) * SPAN, :].astype(f32).T,
                    axis=0,
                    keepdims=True,
                )
                for h in range(HEADS)
            ],
            axis=1,
        )
        dq[...] = jnp.zeros_like(dq)

        def visit(carry, idxs, masked):
            k = rows_of(kv, idxs, 0)
            v = rows_of(kv, idxs, WIDTH)
            s = lax.dot_general(k, qs[j], NT, preferred_element_type=f32) * (SCALE * LOG2E)
            p = jnp.exp2(s - total)
            if masked:
                p = jnp.where(causal_mask(), p, 0.0)
            dp = lax.dot_general(v, gs[j], NT, preferred_element_type=f32)
            ds = (p * (dp - delta)).astype(bf16)
            dk = jnp.dot(ds, qs[j], preferred_element_type=f32)
            dv = jnp.dot(p.astype(bf16), gs[j], preferred_element_type=f32)
            for t, i in enumerate(idxs):
                at = pl.ds(pl.multiple_of(i * SPAN, SPAN), SPAN)
                acc[at, :WIDTH] += dk[t * SPAN : (t + 1) * SPAN]
                acc[at, WIDTH:] += dv[t * SPAN : (t + 1) * SPAN]
            dq[...] += lax.dot_general(k, ds, TN, preferred_element_type=f32)
            return carry

        walk(kb, bc, lst, b, chip, core, visit, 0)
        row = pl.ds(pl.multiple_of((j % 2) * SPAN, SPAN), SPAN)
        for h in range(HEADS):
            piece = dq[:, h * SPAN : (h + 1) * SPAN].T * SCALE

            @pl.when(j < 2)
            def _():
                dq_own[row, h * WIDTH : (h + 1) * WIDTH] = piece

            @pl.when(j >= 2)
            def _():
                dq_sib[row, h * WIDTH : (h + 1) * WIDTH] = piece

        return 0

    lax.fori_loop(0, 4, per_block, 0)
    dkv[:, :WIDTH] = (acc[:, :WIDTH] * SCALE).astype(bf16)
    dkv[:, WIDTH:] = acc[:, WIDTH:].astype(bf16)


def per_device(queries, keys, values, d_y, w_out, key_blocks, block_count):
    chips = lax.axis_size("y") * lax.axis_size("x")
    tok = keys.shape[0]
    swap = [(0, 1), (1, 0)]
    smem = pl.BlockSpec(memory_space=pltpu.SMEM)
    vmem = pl.BlockSpec(memory_space=pltpu.VMEM)
    params = pltpu.CompilerParams(vmem_limit_bytes=48 * 2**20)

    d_y_all = lax.all_gather(d_y, "head", axis=1, tiled=True)
    q_sib = lax.ppermute(queries, "core", swap)
    kv_mine = jnp.concatenate([keys, values], axis=1)
    kv = lax.all_to_all(
        jnp.broadcast_to(kv_mine[None], (chips,) + kv_mine.shape), CHIP_AXES, 0, 0
    ).reshape(chips * tok, 2 * WIDTH)

    stats = pl.pallas_call(
        forward_kernel,
        out_shape=jax.ShapeDtypeStruct((4, WIDTH + 8, ROWS), f32),
        in_specs=[smem, smem, vmem, vmem, vmem],
        out_specs=vmem,
        scratch_shapes=[
            pltpu.VMEM((4, ROWS, WIDTH), bf16),
            pltpu.VMEM((WIDTH, ROWS), f32),
            pltpu.SMEM((32,), jnp.int32),
        ],
        compiler_params=params,
        cost_estimate=pl.CostEstimate(
            flops=6 * 10**9, bytes_accessed=4 * 2**20, transcendentals=4 * 10**6
        ),
        name="forward_statistics",
    )(key_blocks, block_count, queries, q_sib, kv)
    stats_sib = lax.ppermute(stats, "core", swap)

    att_grad = lax.dot_general(d_y_all, w_out, NT, preferred_element_type=f32).astype(bf16)
    grad_sib = lax.ppermute(att_grad, "core", swap)

    dq_own, dq_sib, dkv = pl.pallas_call(
        backward_kernel,
        out_shape=(
            jax.ShapeDtypeStruct((tok, ROWS), f32),
            jax.ShapeDtypeStruct((tok, ROWS), f32),
            jax.ShapeDtypeStruct((chips * tok, 2 * WIDTH), bf16),
        ),
        in_specs=[smem, smem] + [vmem] * 7,
        out_specs=(vmem, vmem, vmem),
        scratch_shapes=[
            pltpu.VMEM((4, ROWS, WIDTH), bf16),
            pltpu.VMEM((4, ROWS, WIDTH), bf16),
            pltpu.VMEM((WIDTH, ROWS), f32),
            pltpu.VMEM((chips * tok, 2 * WIDTH), f32),
            pltpu.SMEM((32,), jnp.int32),
        ],
        compiler_params=params,
        cost_estimate=pl.CostEstimate(
            flops=10 * 10**9, bytes_accessed=8 * 2**20, transcendentals=4 * 10**6
        ),
        name="backward_gradients",
    )(key_blocks, block_count, queries, q_sib, att_grad, grad_sib, kv, stats, stats_sib)

    d_queries = (dq_own + lax.ppermute(dq_sib, "core", swap)).astype(bf16)
    parts = lax.all_to_all(dkv.reshape(chips, tok, 2 * WIDTH), CHIP_AXES, 0, 0)
    summed = jnp.sum(parts.astype(f32), axis=0).astype(bf16)
    return d_queries, summed[:, :WIDTH], summed[:, WIDTH:]


def solution(mesh):
    ctx, head = mesh.devices.shape
    side = math.isqrt(ctx // 2)
    grid = Mesh(mesh.devices.reshape(side, side, 2, head), ("y", "x", "core", "head"))
    ctx_axes = ("y", "x", "core")
    rows = P(ctx_axes, "head")
    return jax.shard_map(
        per_device,
        mesh=grid,
        in_specs=(rows, rows, rows, rows, P("head", None), P(), P()),
        out_specs=(rows, rows, rows),
        check_vma=False,
    )
```

```python
import functools
import math

import jax
import jax.numpy as jnp
from jax import lax
from jax.experimental import pallas as pl
from jax.experimental.pallas import tpu as pltpu
from jax.sharding import Mesh
from jax.sharding import PartitionSpec as P

WIDTH = 128
SPAN = 128
HEADS = 4
ROWS = HEADS * SPAN
SCALE = 1.0 / math.sqrt(WIDTH)
LOG2E = 1.4426950408889634
NEG = -1e30
TILE = 4
CHIP_AXES = ("y", "x")
NT = (((1,), (1,)), ((), ()))
TN = (((0,), (0,)), ((), ()))
f32 = jnp.float32
bf16 = jnp.bfloat16


def my_chip():
    return lax.axis_index("y") * lax.axis_size("x") + lax.axis_index("x")


def query_block(j, chip, core):
    side = jnp.where(j < 2, core, 1 - core)
    return 4 * chip + 2 * side + j % 2


def stack_heads(dst, own, sib):
    for j in range(4):
        src = own if j < 2 else sib
        for h in range(HEADS):
            dst[j, h * SPAN : (h + 1) * SPAN, :] = src[
                (j % 2) * SPAN : (j % 2 + 1) * SPAN, h * WIDTH : (h + 1) * WIDTH
            ]


def list_blocks(kb, bc, lst, b, core):
    def step(s, n):
        blk = kb[b, s]
        lst[n] = 2 * (blk // 4) + blk % 2
        return n + jnp.where((blk // 2) % 2 == core, 1, 0)

    n = lax.fori_loop(1, bc[b], step, 0)
    for t in range(TILE):
        lst[n + t] = 2 * (b // 4) + b % 2
    return n


def rows_of(ref, idxs, lo):
    parts = [
        ref[pl.ds(pl.multiple_of(i * SPAN, SPAN), SPAN), lo : lo + WIDTH] for i in idxs
    ]
    return parts[0] if len(parts) == 1 else jnp.concatenate(parts, axis=0)


def hide(x, limits, fill):
    key = lax.broadcasted_iota(jnp.int32, (SPAN, ROWS), 0)
    qry = lax.broadcasted_iota(jnp.int32, (SPAN, ROWS), 1) % SPAN
    parts = [
        jnp.where(key - qry <= limit, x[t * SPAN : (t + 1) * SPAN], fill)
        for t, limit in enumerate(limits)
    ]
    return jnp.concatenate(parts, axis=0)


def walk(kb, bc, lst, b, core, visit, carry):
    n = list_blocks(kb, bc, lst, b, core)
    has_diag = jnp.where((b // 2) % 2 == core, 1, 0)
    tiles = n // TILE
    done = tiles * TILE
    rest = n - done
    left = rest + has_diag
    carry = lax.fori_loop(
        0, tiles, lambda t, c: visit(c, [lst[t * TILE + i] for i in range(TILE)], None), carry
    )

    def last(count):
        def run(c):
            limits = [
                jnp.where(t < rest, SPAN, jnp.where(t == rest, has_diag * 2 * SPAN, 0) - 2 * SPAN)
                for t in range(count)
            ]
            return visit(c, [lst[done + t] for t in range(count)], limits)

        return run

    def some(c):
        return lax.cond(left <= TILE // 2, last(TILE // 2), last(TILE), c)

    return lax.cond(left > 0, some, lambda c: c, carry)


def forward_kernel(kb, bc, q_own, q_sib, kv, out, qs, qt, acc, lst):
    chip, core = my_chip(), lax.axis_index("core")
    stack_heads(qs, q_own, q_sib)

    def per_block(j, _):
        b = query_block(j, chip, core)
        qt[...] = qs[j].T
        acc[...] = jnp.zeros_like(acc)

        def visit(carry, idxs, limits):
            m, l, l_b = carry
            k = rows_of(kv, idxs, 0)
            v = rows_of(kv, idxs, WIDTH)
            s = jnp.dot(k, qt[...], preferred_element_type=f32) * (SCALE * LOG2E)
            if limits is not None:
                s = hide(s, limits, NEG)
            m_new = jnp.maximum(m, jnp.max(s, axis=0, keepdims=True))
            alpha = jnp.exp2(m - m_new)
            p = jnp.exp2(s - m_new)
            p_b = p.astype(bf16)
            o = lax.dot_general(v, p_b, TN, preferred_element_type=f32)
            acc[...] = acc[...] * alpha + o
            return (
                m_new,
                l * alpha + jnp.sum(p, axis=0, keepdims=True),
                l_b * alpha + jnp.sum(p_b.astype(f32), axis=0, keepdims=True),
            )

        zero = jnp.zeros((1, ROWS), f32)
        m, l, l_b = walk(
            kb, bc, lst, b, core, visit, (jnp.full((1, ROWS), NEG, f32), zero, zero)
        )
        out[j, :WIDTH, :] = acc[...]
        out[j, WIDTH : WIDTH + 8, :] = jnp.concatenate(
            [m, l, l_b, jnp.zeros((5, ROWS), f32)], axis=0
        )
        return 0

    lax.fori_loop(0, 4, per_block, 0)


def backward_kernel(
    kb, bc, q_own, q_sib, g_own, g_sib, kv, st_own, st_sib,
    dq_own, dq_sib, dkv,
    qs, gs, qt, gt, dq, acc, lst,
):
    chip, core = my_chip(), lax.axis_index("core")
    stack_heads(qs, q_own, q_sib)
    stack_heads(gs, g_own, g_sib)
    acc[...] = jnp.zeros_like(acc)

    def per_block(j, _):
        b = query_block(j, chip, core)
        peer = (j + 2) % 4
        qt[...] = qs[j].T
        gt[...] = gs[j].T
        m0, l0, n0 = (st_own[j, WIDTH + i : WIDTH + i + 1, :] for i in range(3))
        m1, l1, n1 = (st_sib[peer, WIDTH + i : WIDTH + i + 1, :] for i in range(3))
        m = jnp.maximum(m0, m1)
        a0, a1 = jnp.exp2(m0 - m), jnp.exp2(m1 - m)
        total = m + jnp.log(l0 * a0 + l1 * a1) * LOG2E
        o = st_own[j, :WIDTH, :] * a0 + st_sib[peer, :WIDTH, :] * a1
        delta = jnp.sum(o * gt[...].astype(f32), axis=0, keepdims=True) / (n0 * a0 + n1 * a1)
        dq[...] = jnp.zeros_like(dq)

        def visit(carry, idxs, limits):
            k = rows_of(kv, idxs, 0)
            v = rows_of(kv, idxs, WIDTH)
            s = jnp.dot(k, qt[...], preferred_element_type=f32) * (SCALE * LOG2E)
            p = jnp.exp2(s - total)
            if limits is not None:
                p = hide(p, limits, 0.0)
            dp = jnp.dot(v, gt[...], preferred_element_type=f32)
            ds = (p * (dp - delta)).astype(bf16)
            dk = jnp.dot(ds, qs[j], preferred_element_type=f32)
            dv = jnp.dot(p.astype(bf16), gs[j], preferred_element_type=f32)
            for t, i in enumerate(idxs):
                at = pl.ds(pl.multiple_of(i * SPAN, SPAN), SPAN)
                acc[at, :WIDTH] += dk[t * SPAN : (t + 1) * SPAN]
                acc[at, WIDTH:] += dv[t * SPAN : (t + 1) * SPAN]
            dq[...] += lax.dot_general(k, ds, TN, preferred_element_type=f32)
            return carry

        walk(kb, bc, lst, b, core, visit, 0)
        row = pl.ds(pl.multiple_of((j % 2) * SPAN, SPAN), SPAN)
        for h in range(HEADS):
            piece = (dq[:, h * SPAN : (h + 1) * SPAN] * SCALE).astype(bf16).T

            @pl.when(j < 2)
            def _():
                dq_own[row, h * WIDTH : (h + 1) * WIDTH] = piece

            @pl.when(j >= 2)
            def _():
                dq_sib[row, h * WIDTH : (h + 1) * WIDTH] = piece

        return 0

    lax.fori_loop(0, 4, per_block, 0)
    dkv[:, :WIDTH] = (acc[:, :WIDTH] * SCALE).astype(bf16)
    dkv[:, WIDTH:] = acc[:, WIDTH:].astype(bf16)


def per_device(queries, keys, values, d_y, w_out, key_blocks, block_count):
    chips = lax.axis_size("y") * lax.axis_size("x")
    tok = keys.shape[0]
    swap = [(0, 1), (1, 0)]
    smem = pl.BlockSpec(memory_space=pltpu.SMEM)
    vmem = pl.BlockSpec(memory_space=pltpu.VMEM)
    params = pltpu.CompilerParams(vmem_limit_bytes=48 * 2**20)

    d_y_all = lax.all_gather(d_y, "head", axis=1, tiled=True)
    q_sib = lax.ppermute(queries, "core", swap)
    kv_mine = jnp.concatenate([keys, values], axis=1)
    kv = lax.all_to_all(
        jnp.broadcast_to(kv_mine[None], (chips,) + kv_mine.shape), CHIP_AXES, 0, 0
    ).reshape(chips * tok, 2 * WIDTH)

    stats = pl.pallas_call(
        forward_kernel,
        out_shape=jax.ShapeDtypeStruct((4, WIDTH + 8, ROWS), f32),
        in_specs=[smem, smem, vmem, vmem, vmem],
        out_specs=vmem,
        scratch_shapes=[
            pltpu.VMEM((4, ROWS, WIDTH), bf16),
            pltpu.VMEM((WIDTH, ROWS), bf16),
            pltpu.VMEM((WIDTH, ROWS), f32),
            pltpu.SMEM((40,), jnp.int32),
        ],
        compiler_params=params,
        cost_estimate=pl.CostEstimate(
            flops=6 * 10**9, bytes_accessed=4 * 2**20, transcendentals=4 * 10**6
        ),
        name="forward_statistics",
    )(key_blocks, block_count, queries, q_sib, kv)
    stats_sib = lax.ppermute(stats, "core", swap)

    att_grad = lax.dot_general(d_y_all, w_out, NT, preferred_element_type=f32).astype(bf16)
    grad_sib = lax.ppermute(att_grad, "core", swap)

    dq_own, dq_sib, dkv = pl.pallas_call(
        backward_kernel,
        out_shape=(
            jax.ShapeDtypeStruct((tok, ROWS), bf16),
            jax.ShapeDtypeStruct((tok, ROWS), bf16),
            jax.ShapeDtypeStruct((chips * tok, 2 * WIDTH), bf16),
        ),
        in_specs=[smem, smem] + [vmem] * 7,
        out_specs=(vmem, vmem, vmem),
        scratch_shapes=[
            pltpu.VMEM((4, ROWS, WIDTH), bf16),
            pltpu.VMEM((4, ROWS, WIDTH), bf16),
            pltpu.VMEM((WIDTH, ROWS), bf16),
            pltpu.VMEM((WIDTH, ROWS), bf16),
            pltpu.VMEM((WIDTH, ROWS), f32),
            pltpu.VMEM((chips * tok, 2 * WIDTH), f32),
            pltpu.SMEM((40,), jnp.int32),
        ],
        compiler_params=params,
        cost_estimate=pl.CostEstimate(
            flops=10 * 10**9, bytes_accessed=8 * 2**20, transcendentals=4 * 10**6
        ),
        name="backward_gradients",
    )(key_blocks, block_count, queries, q_sib, att_grad, grad_sib, kv, stats, stats_sib)

    d_queries = dq_own + lax.ppermute(dq_sib, "core", swap)
    parts = lax.all_to_all(dkv.reshape(chips, tok, 2 * WIDTH), CHIP_AXES, 0, 0)
    summed = jnp.sum(parts.astype(f32), axis=0).astype(bf16)
    return d_queries, summed[:, :WIDTH], summed[:, WIDTH:]


def solution(mesh):
    ctx, head = mesh.devices.shape
    side = math.isqrt(ctx // 2)
    grid = Mesh(mesh.devices.reshape(side, side, 2, head), ("y", "x", "core", "head"))
    ctx_axes = ("y", "x", "core")
    rows = P(ctx_axes, "head")
    return jax.shard_map(
        per_device,
        mesh=grid,
        in_specs=(rows, rows, rows, rows, P("head", None), P(), P()),
        out_specs=(rows, rows, rows),
        check_vma=False,
    )
```

```python
import functools
import math

import jax
import jax.numpy as jnp
from jax import lax
from jax.experimental import pallas as pl
from jax.experimental.pallas import tpu as pltpu
from jax.sharding import Mesh
from jax.sharding import PartitionSpec as P

WIDTH = 128
SPAN = 128
HEADS = 4
ROWS = HEADS * SPAN
SCALE = 1.0 / math.sqrt(WIDTH)
LOG2E = 1.4426950408889634
NEG = -1e30
TILE = 4
CHIP_AXES = ("y", "x")
TOKEN_AXES = ("y", "x", "core")
NT = (((1,), (1,)), ((), ()))
TN = (((0,), (0,)), ((), ()))
f32 = jnp.float32
bf16 = jnp.bfloat16


def my_chip():
    return lax.axis_index("y") * lax.axis_size("x") + lax.axis_index("x")


def query_block(j, chip, core):
    side = jnp.where(j < 2, core, 1 - core)
    chips = lax.axis_size("y") * lax.axis_size("x")
    holder = jnp.where(side == 0, chip, chips - 1 - chip)
    return 4 * holder + 2 * side + j % 2


def stack_heads(dst, own, sib):
    for j in range(4):
        src = own if j < 2 else sib
        for h in range(HEADS):
            dst[j, h * SPAN : (h + 1) * SPAN, :] = src[
                (j % 2) * SPAN : (j % 2 + 1) * SPAN, h * WIDTH : (h + 1) * WIDTH
            ]


def list_blocks(kb, bc, lst, b, core):
    def step(s, n):
        blk = kb[b, s]
        lst[n] = 2 * (blk // 4) + blk % 2
        return n + jnp.where((blk // 2) % 2 == core, 1, 0)

    n = lax.fori_loop(1, bc[b], step, 0)
    for t in range(TILE):
        lst[n + t] = 2 * (b // 4) + b % 2
    return n


def rows_of(ref, idxs, lo):
    parts = [
        ref[pl.ds(pl.multiple_of(i * SPAN, SPAN), SPAN), lo : lo + WIDTH] for i in idxs
    ]
    return parts[0] if len(parts) == 1 else jnp.concatenate(parts, axis=0)


def hide(x, limits, fill):
    key = lax.broadcasted_iota(jnp.int32, (SPAN, ROWS), 0)
    qry = lax.broadcasted_iota(jnp.int32, (SPAN, ROWS), 1) % SPAN
    parts = [
        jnp.where(key - qry <= limit, x[t * SPAN : (t + 1) * SPAN], fill)
        for t, limit in enumerate(limits)
    ]
    return jnp.concatenate(parts, axis=0)


def walk(kb, bc, lst, b, core, visit, carry):
    n = list_blocks(kb, bc, lst, b, core)
    has_diag = jnp.where((b // 2) % 2 == core, 1, 0)
    tiles = n // TILE
    done = tiles * TILE
    rest = n - done
    left = rest + has_diag
    carry = lax.fori_loop(
        0, tiles, lambda t, c: visit(c, [lst[t * TILE + i] for i in range(TILE)], None), carry
    )

    def last(count):
        def run(c):
            limits = [
                jnp.where(t < rest, SPAN, jnp.where(t == rest, has_diag * 2 * SPAN, 0) - 2 * SPAN)
                for t in range(count)
            ]
            return visit(c, [lst[done + t] for t in range(count)], limits)

        return run

    def some(c):
        return lax.cond(left <= TILE // 2, last(TILE // 2), last(TILE), c)

    return lax.cond(left > 0, some, lambda c: c, carry)


def forward_kernel(kb, bc, q_own, q_sib, kv, out, qs, qt, acc, lst):
    chip, core = my_chip(), lax.axis_index("core")
    stack_heads(qs, q_own, q_sib)

    def per_block(j, _):
        b = query_block(j, chip, core)
        qt[...] = qs[j].T
        acc[...] = jnp.zeros_like(acc)

        def visit(carry, idxs, limits):
            m, l, l_b = carry
            k = rows_of(kv, idxs, 0)
            v = rows_of(kv, idxs, WIDTH)
            s = jnp.dot(k, qt[...], preferred_element_type=f32) * (SCALE * LOG2E)
            if limits is not None:
                s = hide(s, limits, NEG)
            m_new = jnp.maximum(m, jnp.max(s, axis=0, keepdims=True))
            alpha = jnp.exp2(m - m_new)
            p = jnp.exp2(s - m_new)
            p_b = p.astype(bf16)
            o = lax.dot_general(v, p_b, TN, preferred_element_type=f32)
            acc[...] = acc[...] * alpha + o
            return (
                m_new,
                l * alpha + jnp.sum(p, axis=0, keepdims=True),
                l_b * alpha + jnp.sum(p_b.astype(f32), axis=0, keepdims=True),
            )

        zero = jnp.zeros((1, ROWS), f32)
        m, l, l_b = walk(
            kb, bc, lst, b, core, visit, (jnp.full((1, ROWS), NEG, f32), zero, zero)
        )
        out[j, :WIDTH, :] = acc[...]
        out[j, WIDTH : WIDTH + 8, :] = jnp.concatenate(
            [m, l, l_b, jnp.zeros((5, ROWS), f32)], axis=0
        )
        return 0

    lax.fori_loop(0, 4, per_block, 0)


def backward_kernel(
    kb, bc, q_own, q_sib, g_own, g_sib, kv, st_own, st_sib,
    dq_own, dq_sib, dkv,
    qs, gs, qt, gt, dq, acc, lst,
):
    chip, core = my_chip(), lax.axis_index("core")
    stack_heads(qs, q_own, q_sib)
    stack_heads(gs, g_own, g_sib)
    acc[...] = jnp.zeros_like(acc)

    def per_block(j, _):
        b = query_block(j, chip, core)
        peer = (j + 2) % 4
        qt[...] = qs[j].T
        gt[...] = gs[j].T
        m0, l0, n0 = (st_own[j, WIDTH + i : WIDTH + i + 1, :] for i in range(3))
        m1, l1, n1 = (st_sib[peer, WIDTH + i : WIDTH + i + 1, :] for i in range(3))
        m = jnp.maximum(m0, m1)
        a0, a1 = jnp.exp2(m0 - m), jnp.exp2(m1 - m)
        total = m + jnp.log(l0 * a0 + l1 * a1) * LOG2E
        o = st_own[j, :WIDTH, :] * a0 + st_sib[peer, :WIDTH, :] * a1
        delta = jnp.sum(o * gt[...].astype(f32), axis=0, keepdims=True) / (n0 * a0 + n1 * a1)
        dq[...] = jnp.zeros_like(dq)

        def visit(carry, idxs, limits):
            k = rows_of(kv, idxs, 0)
            v = rows_of(kv, idxs, WIDTH)
            s = jnp.dot(k, qt[...], preferred_element_type=f32) * (SCALE * LOG2E)
            p = jnp.exp2(s - total)
            if limits is not None:
                p = hide(p, limits, 0.0)
            dp = jnp.dot(v, gt[...], preferred_element_type=f32)
            ds = (p * (dp - delta)).astype(bf16)
            dk = jnp.dot(ds, qs[j], preferred_element_type=f32)
            dv = jnp.dot(p.astype(bf16), gs[j], preferred_element_type=f32)
            for t, i in enumerate(idxs):
                at = pl.ds(pl.multiple_of(i * SPAN, SPAN), SPAN)
                acc[at, :WIDTH] += dk[t * SPAN : (t + 1) * SPAN]
                acc[at, WIDTH:] += dv[t * SPAN : (t + 1) * SPAN]
            dq[...] += lax.dot_general(k, ds, TN, preferred_element_type=f32)
            return carry

        walk(kb, bc, lst, b, core, visit, 0)
        row = pl.ds(pl.multiple_of((j % 2) * SPAN, SPAN), SPAN)
        for h in range(HEADS):
            piece = (dq[:, h * SPAN : (h + 1) * SPAN] * SCALE).astype(bf16).T

            @pl.when(j < 2)
            def _():
                dq_own[row, h * WIDTH : (h + 1) * WIDTH] = piece

            @pl.when(j >= 2)
            def _():
                dq_sib[row, h * WIDTH : (h + 1) * WIDTH] = piece

        return 0

    lax.fori_loop(0, 4, per_block, 0)
    dkv[:, :WIDTH] = (acc[:, :WIDTH] * SCALE).astype(bf16)
    dkv[:, WIDTH:] = acc[:, WIDTH:].astype(bf16)


def per_device(queries, keys, values, d_y, w_out, key_blocks, block_count):
    chips = lax.axis_size("y") * lax.axis_size("x")
    tok = keys.shape[0]
    swap = [(0, 1), (1, 0)]
    smem = pl.BlockSpec(memory_space=pltpu.SMEM)
    vmem = pl.BlockSpec(memory_space=pltpu.VMEM)
    params = pltpu.CompilerParams(vmem_limit_bytes=48 * 2**20)

    fold = [
        (2 * i + c, 2 * i if c == 0 else 2 * (chips - 1 - i) + 1)
        for i in range(chips)
        for c in range(2)
    ]
    d_y = lax.ppermute(d_y, TOKEN_AXES, fold)
    d_y_all = lax.all_gather(d_y, "head", axis=1, tiled=True)
    queries = lax.ppermute(queries, TOKEN_AXES, fold)
    q_sib = lax.ppermute(queries, "core", swap)
    kv_mine = jnp.concatenate([keys, values], axis=1)
    kv = lax.all_to_all(
        jnp.broadcast_to(kv_mine[None], (chips,) + kv_mine.shape), CHIP_AXES, 0, 0
    ).reshape(chips * tok, 2 * WIDTH)

    stats = pl.pallas_call(
        forward_kernel,
        out_shape=jax.ShapeDtypeStruct((4, WIDTH + 8, ROWS), f32),
        in_specs=[smem, smem, vmem, vmem, vmem],
        out_specs=vmem,
        scratch_shapes=[
            pltpu.VMEM((4, ROWS, WIDTH), bf16),
            pltpu.VMEM((WIDTH, ROWS), bf16),
            pltpu.VMEM((WIDTH, ROWS), f32),
            pltpu.SMEM((40,), jnp.int32),
        ],
        compiler_params=params,
        cost_estimate=pl.CostEstimate(
            flops=6 * 10**9, bytes_accessed=4 * 2**20, transcendentals=4 * 10**6
        ),
        name="forward_statistics",
    )(key_blocks, block_count, queries, q_sib, kv)
    stats_sib = lax.ppermute(stats, "core", swap)

    att_grad = lax.dot_general(d_y_all, w_out, NT, preferred_element_type=f32).astype(bf16)
    grad_sib = lax.ppermute(att_grad, "core", swap)

    dq_own, dq_sib, dkv = pl.pallas_call(
        backward_kernel,
        out_shape=(
            jax.ShapeDtypeStruct((tok, ROWS), bf16),
            jax.ShapeDtypeStruct((tok, ROWS), bf16),
            jax.ShapeDtypeStruct((chips * tok, 2 * WIDTH), bf16),
        ),
        in_specs=[smem, smem] + [vmem] * 7,
        out_specs=(vmem, vmem, vmem),
        scratch_shapes=[
            pltpu.VMEM((4, ROWS, WIDTH), bf16),
            pltpu.VMEM((4, ROWS, WIDTH), bf16),
            pltpu.VMEM((WIDTH, ROWS), bf16),
            pltpu.VMEM((WIDTH, ROWS), bf16),
            pltpu.VMEM((WIDTH, ROWS), f32),
            pltpu.VMEM((chips * tok, 2 * WIDTH), f32),
            pltpu.SMEM((40,), jnp.int32),
        ],
        compiler_params=params,
        cost_estimate=pl.CostEstimate(
            flops=10 * 10**9, bytes_accessed=8 * 2**20, transcendentals=4 * 10**6
        ),
        name="backward_gradients",
    )(key_blocks, block_count, queries, q_sib, att_grad, grad_sib, kv, stats, stats_sib)

    d_queries = lax.ppermute(dq_own + lax.ppermute(dq_sib, "core", swap), TOKEN_AXES, fold)
    parts = lax.all_to_all(dkv.reshape(chips, tok, 2 * WIDTH), CHIP_AXES, 0, 0)
    summed = jnp.sum(parts.astype(f32), axis=0).astype(bf16)
    return d_queries, summed[:, :WIDTH], summed[:, WIDTH:]


def solution(mesh):
    ctx, head = mesh.devices.shape
    side = math.isqrt(ctx // 2)
    grid = Mesh(mesh.devices.reshape(side, side, 2, head), ("y", "x", "core", "head"))
    rows = P(TOKEN_AXES, "head")
    return jax.shard_map(
        per_device,
        mesh=grid,
        in_specs=(rows, rows, rows, rows, P("head", None), P(), P()),
        out_specs=(rows, rows, rows),
        check_vma=False,
    )
```

```python
import functools
import math

import jax
import jax.numpy as jnp
from jax import lax
from jax.experimental import pallas as pl
from jax.experimental.pallas import tpu as pltpu
from jax.sharding import Mesh
from jax.sharding import PartitionSpec as P

WIDTH = 128
SPAN = 128
HEADS = 4
ROWS = HEADS * SPAN
SCALE = 1.0 / math.sqrt(WIDTH)
LOG2E = 1.4426950408889634
NEG = -1e30
TILE = 4
CHIP_AXES = ("y", "x")
TOKEN_AXES = ("y", "x", "core")
NT = (((1,), (1,)), ((), ()))
TN = (((0,), (0,)), ((), ()))
f32 = jnp.float32
bf16 = jnp.bfloat16


def my_chip():
    return lax.axis_index("y") * lax.axis_size("x") + lax.axis_index("x")


def query_block(j, chip, core):
    side = jnp.where(j < 2, core, 1 - core)
    chips = lax.axis_size("y") * lax.axis_size("x")
    holder = jnp.where(side == 0, chip, chips - 1 - chip)
    return 4 * holder + 2 * side + j % 2


def head_block(j, h):
    return slice((j % 2) * SPAN, (j % 2 + 1) * SPAN), slice(h * WIDTH, (h + 1) * WIDTH)


def stack_heads(dst, own, sib):
    for j in range(4):
        src = own if j < 2 else sib
        for h in range(HEADS):
            dst[j, h * SPAN : (h + 1) * SPAN, :] = src[head_block(j, h)]


def head_copies(dst, own, sib, sems):
    copies = []
    for j in range(4):
        src = own if j < 2 else sib
        for h in range(HEADS):
            to = dst.at[j, h * SPAN : (h + 1) * SPAN, :]
            copies.append(
                pltpu.make_async_copy(src.at[head_block(j, h)], to, sems.at[j * HEADS + h])
            )
    return copies


def list_blocks(kb, bc, lst, b, core):
    def step(s, n):
        blk = kb[b, s]
        lst[n] = 4 * (blk // 4) + blk % 2
        return n + jnp.where((blk // 2) % 2 == core, 1, 0)

    n = lax.fori_loop(1, bc[b], step, 0)
    for t in range(TILE):
        lst[n + t] = 4 * (b // 4) + b % 2
    return n


def block_rows(i):
    return pl.ds(pl.multiple_of(i * SPAN, SPAN), SPAN)


def rows_of(ref, idxs):
    parts = [ref[block_rows(i), :] for i in idxs]
    return parts[0] if len(parts) == 1 else jnp.concatenate(parts, axis=0)


def hide(x, limits, fill):
    key = lax.broadcasted_iota(jnp.int32, (SPAN, ROWS), 0)
    qry = lax.broadcasted_iota(jnp.int32, (SPAN, ROWS), 1) % SPAN
    parts = [
        jnp.where(key - qry <= limit, x[t * SPAN : (t + 1) * SPAN], fill)
        for t, limit in enumerate(limits)
    ]
    return jnp.concatenate(parts, axis=0)


def walk(kb, bc, lst, b, core, visit, carry):
    n = list_blocks(kb, bc, lst, b, core)
    has_diag = jnp.where((b // 2) % 2 == core, 1, 0)
    tiles = n // TILE
    done = tiles * TILE
    rest = n - done
    left = rest + has_diag
    carry = lax.fori_loop(
        0, tiles, lambda t, c: visit(c, [lst[t * TILE + i] for i in range(TILE)], None), carry
    )

    def last(count):
        def run(c):
            limits = [
                jnp.where(t < rest, SPAN, jnp.where(t == rest, has_diag * 2 * SPAN, 0) - 2 * SPAN)
                for t in range(count)
            ]
            return visit(c, [lst[done + t] for t in range(count)], limits)

        return run

    def some(c):
        return lax.cond(left <= TILE // 2, last(TILE // 2), last(TILE), c)

    return lax.cond(left > 0, some, lambda c: c, carry)


def forward_kernel(kb, bc, q_own, q_sib, kv, out, qs, qt, acc, lst, sems):
    chip, core = my_chip(), lax.axis_index("core")
    copies = head_copies(qs, q_own, q_sib, sems)
    for copy in copies:
        copy.start()
    for copy in copies:
        copy.wait()

    def per_block(j, _):
        b = query_block(j, chip, core)
        qt[...] = qs[j].T
        acc[...] = jnp.zeros_like(acc)

        def visit(carry, idxs, limits):
            m, l, l_b = carry
            k = rows_of(kv, idxs)
            v = rows_of(kv, [i + 2 for i in idxs])
            s = jnp.dot(k, qt[...], preferred_element_type=f32) * (SCALE * LOG2E)
            if limits is not None:
                s = hide(s, limits, NEG)
            m_new = jnp.maximum(m, jnp.max(s, axis=0, keepdims=True))
            alpha = jnp.exp2(m - m_new)
            p = jnp.exp2(s - m_new)
            p_b = p.astype(bf16)
            o = lax.dot_general(v, p_b, TN, preferred_element_type=f32)
            acc[...] = acc[...] * alpha + o
            return (
                m_new,
                l * alpha + jnp.sum(p, axis=0, keepdims=True),
                l_b * alpha + jnp.sum(p_b.astype(f32), axis=0, keepdims=True),
            )

        zero = jnp.zeros((1, ROWS), f32)
        m, l, l_b = walk(
            kb, bc, lst, b, core, visit, (jnp.full((1, ROWS), NEG, f32), zero, zero)
        )
        out[j, :WIDTH, :] = acc[...]
        out[j, WIDTH : WIDTH + 8, :] = jnp.concatenate(
            [m, l, l_b, jnp.zeros((5, ROWS), f32)], axis=0
        )
        return 0

    lax.fori_loop(0, 4, per_block, 0)


def backward_kernel(
    kb, bc, q_own, q_sib, g_own, g_sib, kv, st_own, st_sib,
    dq_own, dq_sib, dkv,
    qs, gs, qt, gt, dq, acc, lst, sems,
):
    chip, core = my_chip(), lax.axis_index("core")
    copies = head_copies(qs, q_own, q_sib, sems)
    for copy in copies:
        copy.start()
    stack_heads(gs, g_own, g_sib)
    acc[...] = jnp.zeros_like(acc)
    for copy in copies:
        copy.wait()

    def per_block(j, _):
        b = query_block(j, chip, core)
        peer = (j + 2) % 4
        qt[...] = qs[j].T
        gt[...] = gs[j].T
        m0, l0, n0 = (st_own[j, WIDTH + i : WIDTH + i + 1, :] for i in range(3))
        m1, l1, n1 = (st_sib[peer, WIDTH + i : WIDTH + i + 1, :] for i in range(3))
        m = jnp.maximum(m0, m1)
        a0, a1 = jnp.exp2(m0 - m), jnp.exp2(m1 - m)
        total = m + jnp.log(l0 * a0 + l1 * a1) * LOG2E
        o = st_own[j, :WIDTH, :] * a0 + st_sib[peer, :WIDTH, :] * a1
        delta = jnp.sum(o * gt[...].astype(f32), axis=0, keepdims=True) / (n0 * a0 + n1 * a1)
        dq[...] = jnp.zeros_like(dq)

        def visit(carry, idxs, limits):
            k = rows_of(kv, idxs)
            v = rows_of(kv, [i + 2 for i in idxs])
            s = jnp.dot(k, qt[...], preferred_element_type=f32) * (SCALE * LOG2E)
            p = jnp.exp2(s - total)
            if limits is not None:
                p = hide(p, limits, 0.0)
            dp = jnp.dot(v, gt[...], preferred_element_type=f32)
            ds = (p * (dp - delta)).astype(bf16)
            dk = jnp.dot(ds, qs[j], preferred_element_type=f32)
            dv = jnp.dot(p.astype(bf16), gs[j], preferred_element_type=f32)
            for t, i in enumerate(idxs):
                acc[block_rows(i), :] += dk[t * SPAN : (t + 1) * SPAN]
                acc[block_rows(i + 2), :] += dv[t * SPAN : (t + 1) * SPAN]
            dq[...] += lax.dot_general(k, ds, TN, preferred_element_type=f32)
            return carry

        walk(kb, bc, lst, b, core, visit, 0)
        row = pl.ds(pl.multiple_of((j % 2) * SPAN, SPAN), SPAN)
        for h in range(HEADS):
            piece = (dq[:, h * SPAN : (h + 1) * SPAN] * SCALE).astype(bf16).T

            @pl.when(j < 2)
            def _():
                dq_own[row, h * WIDTH : (h + 1) * WIDTH] = piece

            @pl.when(j >= 2)
            def _():
                dq_sib[row, h * WIDTH : (h + 1) * WIDTH] = piece

        return 0

    lax.fori_loop(0, 4, per_block, 0)
    for c in range(dkv.shape[0] // (4 * SPAN)):
        mid = (4 * c + 2) * SPAN
        at_k, at_v = slice(mid - 2 * SPAN, mid), slice(mid, mid + 2 * SPAN)
        dkv[at_k, :] = (acc[at_k, :] * SCALE).astype(bf16)
        dkv[at_v, :] = acc[at_v, :].astype(bf16)


def per_device(queries, keys, values, d_y, w_out, key_blocks, block_count):
    chips = lax.axis_size("y") * lax.axis_size("x")
    tok = keys.shape[0]
    swap = [(0, 1), (1, 0)]
    smem = pl.BlockSpec(memory_space=pltpu.SMEM)
    vmem = pl.BlockSpec(memory_space=pltpu.VMEM)
    hbm = pl.BlockSpec(memory_space=pltpu.HBM)
    fold = [
        (2 * i + c, 2 * i if c == 0 else 2 * (chips - 1 - i) + 1)
        for i in range(chips)
        for c in range(2)
    ]

    is_key = lax.broadcasted_iota(jnp.int32, (chips, 2, tok, WIDTH), 1) == 0
    kv_sent = jnp.where(is_key, keys[None, None], values[None, None])
    d_y = lax.ppermute(d_y, TOKEN_AXES, fold)
    d_y, kv_sent = lax.optimization_barrier((d_y, kv_sent))
    d_y_all = lax.all_gather(d_y, "head", axis=1, tiled=True)
    kv = lax.all_to_all(kv_sent, CHIP_AXES, 0, 0).reshape(chips * 2 * tok, WIDTH)
    queries = lax.ppermute(queries, TOKEN_AXES, fold)
    q_sib = lax.ppermute(queries, "core", swap)
    queries, q_sib = (pltpu.with_memory_space_constraint(q, pltpu.HBM) for q in (queries, q_sib))

    stats = pl.pallas_call(
        forward_kernel,
        out_shape=jax.ShapeDtypeStruct((4, WIDTH + 8, ROWS), f32),
        in_specs=[smem, smem, hbm, hbm, vmem],
        out_specs=vmem,
        scratch_shapes=[
            pltpu.VMEM((4, ROWS, WIDTH), bf16),
            pltpu.VMEM((WIDTH, ROWS), bf16),
            pltpu.VMEM((WIDTH, ROWS), f32),
            pltpu.SMEM((40,), jnp.int32),
            pltpu.SemaphoreType.DMA((4 * HEADS,)),
        ],
        compiler_params=pltpu.CompilerParams(vmem_limit_bytes=48 * 2**20),
        cost_estimate=pl.CostEstimate(
            flops=6 * 10**9, bytes_accessed=4 * 2**20, transcendentals=4 * 10**6
        ),
        name="forward_statistics",
    )(key_blocks, block_count, queries, q_sib, kv)
    stats_sib = lax.ppermute(stats, "core", swap)

    att_grad = lax.dot_general(d_y_all, w_out, NT, preferred_element_type=f32).astype(bf16)
    grad_sib = lax.ppermute(att_grad, "core", swap)

    dq_own, dq_sib, dkv = pl.pallas_call(
        backward_kernel,
        out_shape=(
            jax.ShapeDtypeStruct((tok, ROWS), bf16),
            jax.ShapeDtypeStruct((tok, ROWS), bf16),
            jax.ShapeDtypeStruct((chips * 2 * tok, WIDTH), bf16),
        ),
        in_specs=[smem, smem, hbm, hbm] + [vmem] * 5,
        out_specs=(vmem, vmem, vmem),
        scratch_shapes=[
            pltpu.VMEM((4, ROWS, WIDTH), bf16),
            pltpu.VMEM((4, ROWS, WIDTH), bf16),
            pltpu.VMEM((WIDTH, ROWS), bf16),
            pltpu.VMEM((WIDTH, ROWS), bf16),
            pltpu.VMEM((WIDTH, ROWS), f32),
            pltpu.VMEM((chips * 2 * tok, WIDTH), f32),
            pltpu.SMEM((40,), jnp.int32),
            pltpu.SemaphoreType.DMA((4 * HEADS,)),
        ],
        compiler_params=pltpu.CompilerParams(vmem_limit_bytes=48 * 2**20),
        cost_estimate=pl.CostEstimate(
            flops=10 * 10**9, bytes_accessed=8 * 2**20, transcendentals=4 * 10**6
        ),
        name="backward_gradients",
    )(key_blocks, block_count, queries, q_sib, att_grad, grad_sib, kv, stats, stats_sib)

    d_queries = lax.ppermute(dq_own + lax.ppermute(dq_sib, "core", swap), TOKEN_AXES, fold)
    d_queries = pltpu.with_memory_space_constraint(d_queries, pltpu.HBM)
    parts = lax.all_to_all(dkv.reshape(chips, 2 * tok, WIDTH), CHIP_AXES, 0, 0)
    summed = jnp.sum(parts.astype(f32), axis=0).astype(bf16)
    return d_queries, summed[:tok], summed[tok:]


def solution(mesh):
    ctx, head = mesh.devices.shape
    side = math.isqrt(ctx // 2)
    grid = Mesh(mesh.devices.reshape(side, side, 2, head), ("y", "x", "core", "head"))
    rows = P(TOKEN_AXES, "head")
    return jax.shard_map(
        per_device,
        mesh=grid,
        in_specs=(rows, rows, rows, rows, P("head", None), P(), P()),
        out_specs=(rows, rows, rows),
        check_vma=False,
    )
```

```python
import functools
import math

import jax
import jax.numpy as jnp
from jax import lax
from jax.experimental import pallas as pl
from jax.experimental.pallas import tpu as pltpu
from jax.sharding import Mesh
from jax.sharding import PartitionSpec as P

WIDTH = 128
SPAN = 128
HEADS = 4
ROWS = HEADS * SPAN
SCALE = 1.0 / math.sqrt(WIDTH)
LOG2E = 1.4426950408889634
NEG = -1e30
TILE = 4
PARTS = 4
CHIP_AXES = ("y", "x")
TOKEN_AXES = ("y", "x", "core")
NT = (((1,), (1,)), ((), ()))
TN = (((0,), (0,)), ((), ()))
f32 = jnp.float32
bf16 = jnp.bfloat16


def my_chip():
    return lax.axis_index("y") * lax.axis_size("x") + lax.axis_index("x")


def query_block(j, chip, core):
    side = jnp.where(j < 2, core, 1 - core)
    return 4 * chip + 2 * side + j % 2


def head_block(j, h):
    return slice((j % 2) * SPAN, (j % 2 + 1) * SPAN), slice(h * WIDTH, (h + 1) * WIDTH)


def stack_heads(dst, own, sib):
    for j in range(4):
        src = own if j < 2 else sib
        for h in range(HEADS):
            dst[j, h * SPAN : (h + 1) * SPAN, :] = src[head_block(j, h)]


def head_copies(dst, own, sib, sems):
    copies = []
    for j in range(4):
        src = own if j < 2 else sib
        for h in range(HEADS):
            to = dst.at[j, h * SPAN : (h + 1) * SPAN, :]
            copies.append(
                pltpu.make_async_copy(src.at[head_block(j, h)], to, sems.at[j * HEADS + h])
            )
    return copies


def list_blocks(kb, bc, lst, b, core):
    def step(s, n):
        blk = kb[b, s]
        lst[n] = 4 * (blk // 4) + blk % 2
        return n + jnp.where((blk // 2) % 2 == core, 1, 0)

    n = lax.fori_loop(1, bc[b], step, 0)
    for t in range(TILE):
        lst[n + t] = 4 * (b // 4) + b % 2
    return n


def block_rows(i):
    return pl.ds(pl.multiple_of(i * SPAN, SPAN), SPAN)


def rows_of(ref, idxs):
    parts = [ref[block_rows(i), :] for i in idxs]
    return parts[0] if len(parts) == 1 else jnp.concatenate(parts, axis=0)


def hide(x, limits, fill):
    key = lax.broadcasted_iota(jnp.int32, (SPAN, ROWS), 0)
    qry = lax.broadcasted_iota(jnp.int32, (SPAN, ROWS), 1) % SPAN
    parts = [
        jnp.where(key - qry <= limit, x[t * SPAN : (t + 1) * SPAN], fill)
        for t, limit in enumerate(limits)
    ]
    return jnp.concatenate(parts, axis=0)


def walk(kb, bc, lst, b, core, visit, carry):
    n = list_blocks(kb, bc, lst, b, core)
    has_diag = jnp.where((b // 2) % 2 == core, 1, 0)
    tiles = n // TILE
    done = tiles * TILE
    rest = n - done
    left = rest + has_diag
    carry = lax.fori_loop(
        0, tiles, lambda t, c: visit(c, [lst[t * TILE + i] for i in range(TILE)], None), carry
    )

    def last(count):
        def run(c):
            limits = [
                jnp.where(t < rest, SPAN, jnp.where(t == rest, has_diag * 2 * SPAN, 0) - 2 * SPAN)
                for t in range(count)
            ]
            return visit(c, [lst[done + t] for t in range(count)], limits)

        return run

    def some(c):
        return lax.cond(left <= TILE // 2, last(TILE // 2), last(TILE), c)

    return lax.cond(left > 0, some, lambda c: c, carry)


def spread_kernel(keys, values, out, sems):
    chips, tok = out.shape[0], keys.shape[0]
    copies = []
    for c in range(chips):
        copies.append(pltpu.make_async_copy(keys, out.at[c, :tok, :], sems.at[2 * c]))
        copies.append(pltpu.make_async_copy(values, out.at[c, tok:, :], sems.at[2 * c + 1]))
    for copy in copies:
        copy.start()
    for copy in copies:
        copy.wait()


def project_kernel(d_y, w_out, out, y_held, w_held, sems):
    width = y_held.shape[2]
    copies = []
    for i in range(PARTS):
        cols = slice(i * width, (i + 1) * width)
        copies.append(
            (
                pltpu.make_async_copy(d_y.at[:, cols], y_held.at[i], sems.at[2 * i]),
                pltpu.make_async_copy(w_out.at[:, cols], w_held.at[i], sems.at[2 * i + 1]),
            )
        )
    for pair in copies:
        for copy in pair:
            copy.start()
    total = jnp.zeros(out.shape, f32)
    for i, pair in enumerate(copies):
        for copy in pair:
            copy.wait()
        total += lax.dot_general(y_held[i], w_held[i], NT, preferred_element_type=f32)
    out[...] = total.astype(bf16)


def forward_kernel(kb, bc, q_own, q_sib, kv, out, qs, qt, acc, lst, sems):
    chip, core = my_chip(), lax.axis_index("core")
    copies = head_copies(qs, q_own, q_sib, sems)
    for copy in copies:
        copy.start()
    for copy in copies:
        copy.wait()

    def per_block(j, _):
        b = query_block(j, chip, core)
        qt[...] = qs[j].T
        acc[...] = jnp.zeros_like(acc)

        def visit(carry, idxs, limits):
            m, l, l_b = carry
            k = rows_of(kv, idxs)
            v = rows_of(kv, [i + 2 for i in idxs])
            s = jnp.dot(k, qt[...], preferred_element_type=f32) * (SCALE * LOG2E)
            if limits is not None:
                s = hide(s, limits, NEG)
            m_new = jnp.maximum(m, jnp.max(s, axis=0, keepdims=True))
            alpha = jnp.exp2(m - m_new)
            p = jnp.exp2(s - m_new)
            p_b = p.astype(bf16)
            o = lax.dot_general(v, p_b, TN, preferred_element_type=f32)
            acc[...] = acc[...] * alpha + o
            return (
                m_new,
                l * alpha + jnp.sum(p, axis=0, keepdims=True),
                l_b * alpha + jnp.sum(p_b.astype(f32), axis=0, keepdims=True),
            )

        zero = jnp.zeros((1, ROWS), f32)
        m, l, l_b = walk(
            kb, bc, lst, b, core, visit, (jnp.full((1, ROWS), NEG, f32), zero, zero)
        )
        out[j, :WIDTH, :] = acc[...]
        out[j, WIDTH : WIDTH + 8, :] = jnp.concatenate(
            [m, l, l_b, jnp.zeros((5, ROWS), f32)], axis=0
        )
        return 0

    lax.fori_loop(0, 4, per_block, 0)


def backward_kernel(
    kb, bc, q_own, q_sib, g_own, g_sib, kv_in, st_own, st_sib,
    dq_own, dq_sib, dkv,
    qs, gs, qt, gt, dq, kv, acc, held, lst, sems, out_sems,
):
    chip, core = my_chip(), lax.axis_index("core")
    copies = [pltpu.make_async_copy(kv_in, kv, sems.at[4 * HEADS])]
    copies += head_copies(qs, q_own, q_sib, sems)
    for copy in copies:
        copy.start()
    stack_heads(gs, g_own, g_sib)
    acc[...] = jnp.zeros_like(acc)
    for copy in copies:
        copy.wait()

    def per_block(j, _):
        b = query_block(j, chip, core)
        peer = (j + 2) % 4
        qt[...] = qs[j].T
        gt[...] = gs[j].T
        m0, l0, n0 = (st_own[j, WIDTH + i : WIDTH + i + 1, :] for i in range(3))
        m1, l1, n1 = (st_sib[peer, WIDTH + i : WIDTH + i + 1, :] for i in range(3))
        m = jnp.maximum(m0, m1)
        a0, a1 = jnp.exp2(m0 - m), jnp.exp2(m1 - m)
        total = m + jnp.log(l0 * a0 + l1 * a1) * LOG2E
        o = st_own[j, :WIDTH, :] * a0 + st_sib[peer, :WIDTH, :] * a1
        delta = jnp.sum(o * gt[...].astype(f32), axis=0, keepdims=True) / (n0 * a0 + n1 * a1)
        dq[...] = jnp.zeros_like(dq)

        def visit(carry, idxs, limits):
            k = rows_of(kv, idxs)
            v = rows_of(kv, [i + 2 for i in idxs])
            s = jnp.dot(k, qt[...], preferred_element_type=f32) * (SCALE * LOG2E)
            p = jnp.exp2(s - total)
            if limits is not None:
                p = hide(p, limits, 0.0)
            dp = jnp.dot(v, gt[...], preferred_element_type=f32)
            ds = (p * (dp - delta)).astype(bf16)
            dk = jnp.dot(ds, qs[j], preferred_element_type=f32)
            dv = jnp.dot(p.astype(bf16), gs[j], preferred_element_type=f32)
            for t, i in enumerate(idxs):
                acc[block_rows(i), :] += dk[t * SPAN : (t + 1) * SPAN]
                acc[block_rows(i + 2), :] += dv[t * SPAN : (t + 1) * SPAN]
            dq[...] += lax.dot_general(k, ds, TN, preferred_element_type=f32)
            return carry

        walk(kb, bc, lst, b, core, visit, 0)
        row = pl.ds(pl.multiple_of((j % 2) * SPAN, SPAN), SPAN)
        for h in range(HEADS):
            piece = (dq[:, h * SPAN : (h + 1) * SPAN] * SCALE).astype(bf16).T

            @pl.when(j < 2)
            def _():
                dq_own[row, h * WIDTH : (h + 1) * WIDTH] = piece

            @pl.when(j >= 2)
            def _():
                dq_sib[row, h * WIDTH : (h + 1) * WIDTH] = piece

        return 0

    lax.fori_loop(0, 4, per_block, 0)
    chunk = 4 * SPAN
    copies = []
    for c in range(dkv.shape[0] // chunk):
        rows = slice(c * chunk, (c + 1) * chunk)
        at_k, at_v = slice(c * chunk, c * chunk + chunk // 2), slice(c * chunk + chunk // 2, (c + 1) * chunk)
        held[at_k, :] = (acc[at_k, :] * SCALE).astype(bf16)
        held[at_v, :] = acc[at_v, :].astype(bf16)
        copies.append(pltpu.make_async_copy(held.at[rows, :], dkv.at[rows, :], out_sems.at[c]))
        copies[-1].start()
    for copy in copies:
        copy.wait()


def per_device(queries, keys, values, d_y, w_out, key_blocks, block_count):
    chips = lax.axis_size("y") * lax.axis_size("x")
    tok = keys.shape[0]
    swap = [(0, 1), (1, 0)]
    smem = pl.BlockSpec(memory_space=pltpu.SMEM)
    vmem = pl.BlockSpec(memory_space=pltpu.VMEM)
    hbm = pl.BlockSpec(memory_space=pltpu.HBM)
    d_y_all = lax.all_gather(d_y, "head", axis=1, tiled=True)
    kv_sent = pl.pallas_call(
        spread_kernel,
        out_shape=jax.ShapeDtypeStruct((chips, 2 * tok, WIDTH), bf16),
        in_specs=[vmem, vmem],
        out_specs=hbm,
        scratch_shapes=[pltpu.SemaphoreType.DMA((2 * chips,))],
        cost_estimate=pl.CostEstimate(
            flops=0, bytes_accessed=chips * 2 * tok * WIDTH * 2, transcendentals=0
        ),
        name="spread_keys_values",
    )(keys, values)
    kv = lax.all_to_all(kv_sent, CHIP_AXES, 0, 0).reshape(chips * 2 * tok, WIDTH)
    q_sib = lax.ppermute(queries, "core", swap)
    queries, q_sib = (pltpu.with_memory_space_constraint(q, pltpu.HBM) for q in (queries, q_sib))

    stats = pl.pallas_call(
        forward_kernel,
        out_shape=jax.ShapeDtypeStruct((4, WIDTH + 8, ROWS), f32),
        in_specs=[smem, smem, hbm, hbm, vmem],
        out_specs=vmem,
        scratch_shapes=[
            pltpu.VMEM((4, ROWS, WIDTH), bf16),
            pltpu.VMEM((WIDTH, ROWS), bf16),
            pltpu.VMEM((WIDTH, ROWS), f32),
            pltpu.SMEM((40,), jnp.int32),
            pltpu.SemaphoreType.DMA((4 * HEADS,)),
        ],
        compiler_params=pltpu.CompilerParams(vmem_limit_bytes=48 * 2**20),
        cost_estimate=pl.CostEstimate(
            flops=6 * 10**9, bytes_accessed=4 * 2**20, transcendentals=4 * 10**6
        ),
        name="forward_statistics",
    )(key_blocks, block_count, queries, q_sib, kv)
    stats_sib = lax.ppermute(stats, "core", swap)

    att_grad = pl.pallas_call(
        project_kernel,
        out_shape=jax.ShapeDtypeStruct((tok, ROWS), bf16),
        in_specs=[hbm, hbm],
        out_specs=vmem,
        scratch_shapes=[
            pltpu.VMEM((PARTS, tok, w_out.shape[1] // PARTS), bf16),
            pltpu.VMEM((PARTS, w_out.shape[0], w_out.shape[1] // PARTS), bf16),
            pltpu.SemaphoreType.DMA((2 * PARTS,)),
        ],
        compiler_params=pltpu.CompilerParams(vmem_limit_bytes=32 * 2**20),
        cost_estimate=pl.CostEstimate(
            flops=2 * tok * w_out.size, bytes_accessed=6 * 2**20, transcendentals=0
        ),
        name="attention_cotangent",
    )(*(pltpu.with_memory_space_constraint(a, pltpu.HBM) for a in (d_y_all, w_out)))
    grad_sib = lax.ppermute(att_grad, "core", swap)

    dq_own, dq_sib, dkv = pl.pallas_call(
        backward_kernel,
        out_shape=(
            jax.ShapeDtypeStruct((tok, ROWS), bf16),
            jax.ShapeDtypeStruct((tok, ROWS), bf16),
            jax.ShapeDtypeStruct((chips * 2 * tok, WIDTH), bf16),
        ),
        in_specs=[smem, smem, hbm, hbm, vmem, vmem, hbm, vmem, vmem],
        out_specs=(vmem, vmem, hbm),
        scratch_shapes=[
            pltpu.VMEM((4, ROWS, WIDTH), bf16),
            pltpu.VMEM((4, ROWS, WIDTH), bf16),
            pltpu.VMEM((WIDTH, ROWS), bf16),
            pltpu.VMEM((WIDTH, ROWS), bf16),
            pltpu.VMEM((WIDTH, ROWS), f32),
            pltpu.VMEM((chips * 2 * tok, WIDTH), bf16),
            pltpu.VMEM((chips * 2 * tok, WIDTH), f32),
            pltpu.VMEM((chips * 2 * tok, WIDTH), bf16),
            pltpu.SMEM((40,), jnp.int32),
            pltpu.SemaphoreType.DMA((4 * HEADS + 1,)),
            pltpu.SemaphoreType.DMA((chips,)),
        ],
        compiler_params=pltpu.CompilerParams(vmem_limit_bytes=48 * 2**20),
        cost_estimate=pl.CostEstimate(
            flops=10 * 10**9, bytes_accessed=8 * 2**20, transcendentals=4 * 10**6
        ),
        name="backward_gradients",
    )(key_blocks, block_count, queries, q_sib, att_grad, grad_sib, kv, stats, stats_sib)

    d_queries = dq_own + lax.ppermute(dq_sib, "core", swap)
    parts = lax.all_to_all(dkv.reshape(chips, 2 * tok, WIDTH), CHIP_AXES, 0, 0)
    summed = jnp.sum(parts.astype(f32), axis=0).astype(bf16)
    return d_queries, summed[:tok], summed[tok:]


def solution(mesh):
    ctx, head = mesh.devices.shape
    side = math.isqrt(ctx // 2)
    grid = Mesh(mesh.devices.reshape(side, side, 2, head), ("y", "x", "core", "head"))
    rows = P(TOKEN_AXES, "head")
    return jax.shard_map(
        per_device,
        mesh=grid,
        in_specs=(rows, rows, rows, rows, P("head", None), P(), P()),
        out_specs=(rows, rows, rows),
        check_vma=False,
    )
```

```python
import functools
import math

import jax
import jax.numpy as jnp
from jax import lax
from jax.experimental import pallas as pl
from jax.experimental.pallas import tpu as pltpu
from jax.sharding import Mesh
from jax.sharding import PartitionSpec as P

WIDTH = 128
SPAN = 128
HEADS = 4
ROWS = HEADS * SPAN
SCALE = 1.0 / math.sqrt(WIDTH)
LOG2E = 1.4426950408889634
NEG = -1e30
TILE = 4
PARTS = 4
CHIP_AXES = ("y", "x")
TOKEN_AXES = ("y", "x", "core")
NT = (((1,), (1,)), ((), ()))
TN = (((0,), (0,)), ((), ()))
f32 = jnp.float32
bf16 = jnp.bfloat16


def my_chip():
    return lax.axis_index("y") * lax.axis_size("x") + lax.axis_index("x")


def query_block(j, chip, core):
    side = jnp.where(j < 2, core, 1 - core)
    return 4 * chip + 2 * side + j % 2


def head_block(j, h):
    return slice((j % 2) * SPAN, (j % 2 + 1) * SPAN), slice(h * WIDTH, (h + 1) * WIDTH)


def stack_heads(dst, own, sib):
    for j in range(4):
        src = own if j < 2 else sib
        for h in range(HEADS):
            dst[j, h * SPAN : (h + 1) * SPAN, :] = src[head_block(j, h)]


def head_copies(dst, own, sib, sems):
    copies = []
    for j in range(4):
        src = own if j < 2 else sib
        for h in range(HEADS):
            to = dst.at[j, h * SPAN : (h + 1) * SPAN, :]
            copies.append(
                pltpu.make_async_copy(src.at[head_block(j, h)], to, sems.at[j * HEADS + h])
            )
    return copies


def list_blocks(kb, bc, lst, b, core):
    def step(s, n):
        blk = kb[b, s]
        lst[n] = 4 * (blk // 4) + blk % 2
        return n + jnp.where((blk // 2) % 2 == core, 1, 0)

    n = lax.fori_loop(1, bc[b], step, 0)
    for t in range(TILE):
        lst[n + t] = 4 * (b // 4) + b % 2
    return n


def block_rows(i):
    return pl.ds(pl.multiple_of(i * SPAN, SPAN), SPAN)


def rows_of(ref, idxs):
    parts = [ref[block_rows(i), :] for i in idxs]
    return parts[0] if len(parts) == 1 else jnp.concatenate(parts, axis=0)


def hide(x, limits, fill):
    key = lax.broadcasted_iota(jnp.int32, (SPAN, ROWS), 0)
    qry = lax.broadcasted_iota(jnp.int32, (SPAN, ROWS), 1) % SPAN
    parts = [
        jnp.where(key - qry <= limit, x[t * SPAN : (t + 1) * SPAN], fill)
        for t, limit in enumerate(limits)
    ]
    return jnp.concatenate(parts, axis=0)


def walk(kb, bc, lst, b, core, visit, carry):
    n = list_blocks(kb, bc, lst, b, core)
    has_diag = jnp.where((b // 2) % 2 == core, 1, 0)
    tiles = n // TILE
    done = tiles * TILE
    rest = n - done
    left = rest + has_diag
    carry = lax.fori_loop(
        0, tiles, lambda t, c: visit(c, [lst[t * TILE + i] for i in range(TILE)], None), carry
    )

    def last(count):
        def run(c):
            limits = [
                jnp.where(t < rest, SPAN, jnp.where(t == rest, has_diag * 2 * SPAN, 0) - 2 * SPAN)
                for t in range(count)
            ]
            return visit(c, [lst[done + t] for t in range(count)], limits)

        return run

    def some(c):
        return lax.cond(left <= TILE // 2, last(TILE // 2), last(TILE), c)

    return lax.cond(left > 0, some, lambda c: c, carry)


def spread_kernel(keys, values, out, sems):
    chips, tok = out.shape[0], keys.shape[0]
    copies = []
    for c in range(chips):
        copies.append(pltpu.make_async_copy(keys, out.at[c, :tok, :], sems.at[2 * c]))
        copies.append(pltpu.make_async_copy(values, out.at[c, tok:, :], sems.at[2 * c + 1]))
    for copy in copies:
        copy.start()
    for copy in copies:
        copy.wait()


def project_kernel(d_y, w_out, out, y_held, w_held, sems):
    width = y_held.shape[2]
    copies = []
    for i in range(PARTS):
        cols = slice(i * width, (i + 1) * width)
        copies.append(
            (
                pltpu.make_async_copy(d_y.at[:, cols], y_held.at[i], sems.at[2 * i]),
                pltpu.make_async_copy(w_out.at[:, cols], w_held.at[i], sems.at[2 * i + 1]),
            )
        )
    for pair in copies:
        for copy in pair:
            copy.start()
    total = jnp.zeros(out.shape, f32)
    for i, pair in enumerate(copies):
        for copy in pair:
            copy.wait()
        total += lax.dot_general(y_held[i], w_held[i], NT, preferred_element_type=f32)
    out[...] = total.astype(bf16)


def forward_kernel(kb, bc, q_own, q_sib, kv, out, qs, qt, acc, lst, sems):
    chip, core = my_chip(), lax.axis_index("core")
    copies = head_copies(qs, q_own, q_sib, sems)
    for copy in copies:
        copy.start()
    for copy in copies:
        copy.wait()

    def per_block(j, _):
        b = query_block(j, chip, core)
        qt[...] = qs[j].T
        acc[...] = jnp.zeros_like(acc)

        def visit(carry, idxs, limits):
            m, l, l_b = carry
            k = rows_of(kv, idxs)
            v = rows_of(kv, [i + 2 for i in idxs])
            s = jnp.dot(k, qt[...], preferred_element_type=f32) * (SCALE * LOG2E)
            if limits is not None:
                s = hide(s, limits, NEG)
            m_new = jnp.maximum(m, jnp.max(s, axis=0, keepdims=True))
            alpha = jnp.exp2(m - m_new)
            p = jnp.exp2(s - m_new)
            p_b = p.astype(bf16)
            o = lax.dot_general(v, p_b, TN, preferred_element_type=f32)
            acc[...] = acc[...] * alpha + o
            return (
                m_new,
                l * alpha + jnp.sum(p, axis=0, keepdims=True),
                l_b * alpha + jnp.sum(p_b.astype(f32), axis=0, keepdims=True),
            )

        zero = jnp.zeros((1, ROWS), f32)
        m, l, l_b = walk(
            kb, bc, lst, b, core, visit, (jnp.full((1, ROWS), NEG, f32), zero, zero)
        )
        out[j, :WIDTH, :] = acc[...]
        out[j, WIDTH : WIDTH + 8, :] = jnp.concatenate(
            [m, l, l_b, jnp.zeros((5, ROWS), f32)], axis=0
        )
        return 0

    lax.fori_loop(0, 4, per_block, 0)


def backward_kernel(
    kb, bc, q_own, q_sib, g_own, g_sib, kv_in, st_own, st_sib,
    dq_own, dq_sib, dkv,
    qs, gs, qt, gt, dq, kv, acc, held, lst, sems, out_sems,
):
    chip, core = my_chip(), lax.axis_index("core")
    copies = [pltpu.make_async_copy(kv_in, kv, sems.at[4 * HEADS])]
    copies += head_copies(qs, q_own, q_sib, sems)
    for copy in copies:
        copy.start()
    stack_heads(gs, g_own, g_sib)
    acc[...] = jnp.zeros_like(acc)
    for copy in copies:
        copy.wait()

    def per_block(j, _):
        b = query_block(j, chip, core)
        peer = (j + 2) % 4
        qt[...] = qs[j].T
        gt[...] = gs[j].T
        m0, l0, n0 = (st_own[j, WIDTH + i : WIDTH + i + 1, :] for i in range(3))
        m1, l1, n1 = (st_sib[peer, WIDTH + i : WIDTH + i + 1, :] for i in range(3))
        m = jnp.maximum(m0, m1)
        a0, a1 = jnp.exp2(m0 - m), jnp.exp2(m1 - m)
        total = m + jnp.log(l0 * a0 + l1 * a1) * LOG2E
        o = st_own[j, :WIDTH, :] * a0 + st_sib[peer, :WIDTH, :] * a1
        delta = jnp.sum(o * gt[...].astype(f32), axis=0, keepdims=True) / (n0 * a0 + n1 * a1)
        dq[...] = jnp.zeros_like(dq)

        def visit(carry, idxs, limits):
            k = rows_of(kv, idxs)
            v = rows_of(kv, [i + 2 for i in idxs])
            s = jnp.dot(k, qt[...], preferred_element_type=f32) * (SCALE * LOG2E)
            p = jnp.exp2(s - total)
            if limits is not None:
                p = hide(p, limits, 0.0)
            dp = jnp.dot(v, gt[...], preferred_element_type=f32)
            ds = (p * (dp - delta)).astype(bf16)
            dk = jnp.dot(ds, qs[j], preferred_element_type=f32)
            dv = jnp.dot(p.astype(bf16), gs[j], preferred_element_type=f32)
            for t, i in enumerate(idxs):
                acc[block_rows(i), :] += dk[t * SPAN : (t + 1) * SPAN]
                acc[block_rows(i + 2), :] += dv[t * SPAN : (t + 1) * SPAN]
            dq[...] += lax.dot_general(k, ds, TN, preferred_element_type=f32)
            return carry

        walk(kb, bc, lst, b, core, visit, 0)
        row = pl.ds(pl.multiple_of((j % 2) * SPAN, SPAN), SPAN)
        for h in range(HEADS):
            piece = (dq[:, h * SPAN : (h + 1) * SPAN] * SCALE).astype(bf16).T

            @pl.when(j < 2)
            def _():
                dq_own[row, h * WIDTH : (h + 1) * WIDTH] = piece

            @pl.when(j >= 2)
            def _():
                dq_sib[row, h * WIDTH : (h + 1) * WIDTH] = piece

        return 0

    lax.fori_loop(0, 4, per_block, 0)
    half = 2 * SPAN
    copies = []
    for c in range(dkv.shape[0] // half):
        rows = slice(c * half, (c + 1) * half)
        at = 2 * c * half
        held[rows, :WIDTH] = (acc[at : at + half, :] * SCALE).astype(bf16)
        held[rows, WIDTH:] = acc[at + half : at + 2 * half, :].astype(bf16)
        copies.append(pltpu.make_async_copy(held.at[rows, :], dkv.at[rows, :], out_sems.at[c]))
        copies[-1].start()
    for copy in copies:
        copy.wait()


def per_device(queries, keys, values, d_y, w_out, key_blocks, block_count):
    chips = lax.axis_size("y") * lax.axis_size("x")
    tok = keys.shape[0]
    swap = [(0, 1), (1, 0)]
    smem = pl.BlockSpec(memory_space=pltpu.SMEM)
    vmem = pl.BlockSpec(memory_space=pltpu.VMEM)
    hbm = pl.BlockSpec(memory_space=pltpu.HBM)
    d_y_all = lax.all_gather(d_y, "head", axis=1, tiled=True)
    kv_sent = pl.pallas_call(
        spread_kernel,
        out_shape=jax.ShapeDtypeStruct((chips, 2 * tok, WIDTH), bf16),
        in_specs=[vmem, vmem],
        out_specs=hbm,
        scratch_shapes=[pltpu.SemaphoreType.DMA((2 * chips,))],
        cost_estimate=pl.CostEstimate(
            flops=0, bytes_accessed=chips * 2 * tok * WIDTH * 2, transcendentals=0
        ),
        name="spread_keys_values",
    )(keys, values)
    kv = lax.all_to_all(kv_sent, CHIP_AXES, 0, 0).reshape(chips * 2 * tok, WIDTH)
    q_sib = lax.ppermute(queries, "core", swap)
    queries, q_sib = (pltpu.with_memory_space_constraint(q, pltpu.HBM) for q in (queries, q_sib))

    stats = pl.pallas_call(
        forward_kernel,
        out_shape=jax.ShapeDtypeStruct((4, WIDTH + 8, ROWS), f32),
        in_specs=[smem, smem, hbm, hbm, vmem],
        out_specs=vmem,
        scratch_shapes=[
            pltpu.VMEM((4, ROWS, WIDTH), bf16),
            pltpu.VMEM((WIDTH, ROWS), bf16),
            pltpu.VMEM((WIDTH, ROWS), f32),
            pltpu.SMEM((40,), jnp.int32),
            pltpu.SemaphoreType.DMA((4 * HEADS,)),
        ],
        compiler_params=pltpu.CompilerParams(vmem_limit_bytes=48 * 2**20),
        cost_estimate=pl.CostEstimate(
            flops=6 * 10**9, bytes_accessed=4 * 2**20, transcendentals=4 * 10**6
        ),
        name="forward_statistics",
    )(key_blocks, block_count, queries, q_sib, kv)
    stats_sib = lax.ppermute(stats, "core", swap)

    att_grad = pl.pallas_call(
        project_kernel,
        out_shape=jax.ShapeDtypeStruct((tok, ROWS), bf16),
        in_specs=[hbm, hbm],
        out_specs=vmem,
        scratch_shapes=[
            pltpu.VMEM((PARTS, tok, w_out.shape[1] // PARTS), bf16),
            pltpu.VMEM((PARTS, w_out.shape[0], w_out.shape[1] // PARTS), bf16),
            pltpu.SemaphoreType.DMA((2 * PARTS,)),
        ],
        compiler_params=pltpu.CompilerParams(vmem_limit_bytes=32 * 2**20),
        cost_estimate=pl.CostEstimate(
            flops=2 * tok * w_out.size, bytes_accessed=6 * 2**20, transcendentals=0
        ),
        name="attention_cotangent",
    )(*(pltpu.with_memory_space_constraint(a, pltpu.HBM) for a in (d_y_all, w_out)))
    grad_sib = lax.ppermute(att_grad, "core", swap)

    dq_own, dq_sib, dkv = pl.pallas_call(
        backward_kernel,
        out_shape=(
            jax.ShapeDtypeStruct((tok, ROWS), bf16),
            jax.ShapeDtypeStruct((tok, ROWS), bf16),
            jax.ShapeDtypeStruct((chips * tok, 2 * WIDTH), bf16),
        ),
        in_specs=[smem, smem, hbm, hbm, vmem, vmem, hbm, vmem, vmem],
        out_specs=(vmem, vmem, hbm),
        scratch_shapes=[
            pltpu.VMEM((4, ROWS, WIDTH), bf16),
            pltpu.VMEM((4, ROWS, WIDTH), bf16),
            pltpu.VMEM((WIDTH, ROWS), bf16),
            pltpu.VMEM((WIDTH, ROWS), bf16),
            pltpu.VMEM((WIDTH, ROWS), f32),
            pltpu.VMEM((chips * 2 * tok, WIDTH), bf16),
            pltpu.VMEM((chips * 2 * tok, WIDTH), f32),
            pltpu.VMEM((chips * tok, 2 * WIDTH), bf16),
            pltpu.SMEM((40,), jnp.int32),
            pltpu.SemaphoreType.DMA((4 * HEADS + 1,)),
            pltpu.SemaphoreType.DMA((chips,)),
        ],
        compiler_params=pltpu.CompilerParams(vmem_limit_bytes=48 * 2**20),
        cost_estimate=pl.CostEstimate(
            flops=10 * 10**9, bytes_accessed=8 * 2**20, transcendentals=4 * 10**6
        ),
        name="backward_gradients",
    )(key_blocks, block_count, queries, q_sib, att_grad, grad_sib, kv, stats, stats_sib)

    d_queries = dq_own + lax.ppermute(dq_sib, "core", swap)
    parts = lax.all_to_all(dkv.reshape(chips, tok, 2 * WIDTH), CHIP_AXES, 0, 0)
    summed = jnp.sum(parts.astype(f32), axis=0).astype(bf16)
    return d_queries, summed[:, :WIDTH], summed[:, WIDTH:]


def solution(mesh):
    ctx, head = mesh.devices.shape
    side = math.isqrt(ctx // 2)
    grid = Mesh(mesh.devices.reshape(side, side, 2, head), ("y", "x", "core", "head"))
    rows = P(TOKEN_AXES, "head")
    return jax.shard_map(
        per_device,
        mesh=grid,
        in_specs=(rows, rows, rows, rows, P("head", None), P(), P()),
        out_specs=(rows, rows, rows),
        check_vma=False,
    )
```

```python
import functools
import math

import jax
import jax.numpy as jnp
from jax import lax
from jax.experimental import pallas as pl
from jax.experimental.pallas import tpu as pltpu
from jax.sharding import Mesh
from jax.sharding import PartitionSpec as P

WIDTH = 128
SPAN = 128
HEADS = 4
ROWS = HEADS * SPAN
SCALE = 1.0 / math.sqrt(WIDTH)
LOG2E = 1.4426950408889634
NEG = -1e30
TILE = 4
PARTS = 4
CHIP_AXES = ("y", "x")
TOKEN_AXES = ("y", "x", "core")
NT = (((1,), (1,)), ((), ()))
TN = (((0,), (0,)), ((), ()))
f32 = jnp.float32
bf16 = jnp.bfloat16


def my_chip():
    return lax.axis_index("y") * lax.axis_size("x") + lax.axis_index("x")


def query_block(j, chip, core):
    side = jnp.where(j < 2, core, 1 - core)
    return 4 * chip + 2 * side + j % 2


def head_block(j, h):
    return slice((j % 2) * SPAN, (j % 2 + 1) * SPAN), slice(h * WIDTH, (h + 1) * WIDTH)


def stack_heads(dst, own, sib):
    for j in range(4):
        src = own if j < 2 else sib
        for h in range(HEADS):
            dst[j, h * SPAN : (h + 1) * SPAN, :] = src[head_block(j, h)]


def head_copies(dst, own, sib, sems):
    copies = []
    for j in range(4):
        src = own if j < 2 else sib
        for h in range(HEADS):
            to = dst.at[j, h * SPAN : (h + 1) * SPAN, :]
            copies.append(
                pltpu.make_async_copy(src.at[head_block(j, h)], to, sems.at[j * HEADS + h])
            )
    return copies


def list_blocks(kb, bc, lst, b, core, part):
    def step(s, n):
        blk = kb[b, s]
        lst[n] = 2 * (blk // 4)
        return n + jnp.where(blk % 4 == 2 * core + part, 1, 0)

    n = lax.fori_loop(1, bc[b], step, 0)
    for t in range(TILE):
        lst[n + t] = 2 * (b // 4)
    return n


def block_rows(i):
    return pl.ds(pl.multiple_of(i * SPAN, SPAN), SPAN)


def rows_of(ref, idxs):
    parts = [ref[block_rows(i), :] for i in idxs]
    return parts[0] if len(parts) == 1 else jnp.concatenate(parts, axis=0)


def hide(x, limits, fill):
    key = lax.broadcasted_iota(jnp.int32, (SPAN, ROWS), 0)
    qry = lax.broadcasted_iota(jnp.int32, (SPAN, ROWS), 1) % SPAN
    parts = [
        jnp.where(key - qry <= limit, x[t * SPAN : (t + 1) * SPAN], fill)
        for t, limit in enumerate(limits)
    ]
    return jnp.concatenate(parts, axis=0)


def walk(kb, bc, lst, b, core, part, visit, carry):
    n = list_blocks(kb, bc, lst, b, core, part)
    has_diag = jnp.where(b % 4 == 2 * core + part, 1, 0)
    tiles = n // TILE
    done = tiles * TILE
    rest = n - done
    left = rest + has_diag
    carry = lax.fori_loop(
        0, tiles, lambda t, c: visit(c, [lst[t * TILE + i] for i in range(TILE)], None), carry
    )

    def last(count):
        def run(c):
            limits = [
                jnp.where(t < rest, SPAN, jnp.where(t == rest, has_diag * 2 * SPAN, 0) - 2 * SPAN)
                for t in range(count)
            ]
            return visit(c, [lst[done + t] for t in range(count)], limits)

        return run

    def some(c):
        return lax.cond(left <= TILE // 2, last(TILE // 2), last(TILE), c)

    return lax.cond(left > 0, some, lambda c: c, carry)


def spread_kernel(part, keys, values, out, sems):
    chips = out.shape[0]
    rows = slice(part * SPAN, (part + 1) * SPAN)
    copies = []
    for c in range(chips):
        copies.append(pltpu.make_async_copy(keys.at[rows, :], out.at[c, :SPAN, :], sems.at[2 * c]))
        copies.append(pltpu.make_async_copy(values.at[rows, :], out.at[c, SPAN:, :], sems.at[2 * c + 1]))
    for copy in copies:
        copy.start()
    for copy in copies:
        copy.wait()


def project_kernel(d_y, w_out, out, y_held, w_held, sems):
    width = y_held.shape[2]
    copies = []
    for i in range(PARTS):
        cols = slice(i * width, (i + 1) * width)
        copies.append(
            (
                pltpu.make_async_copy(d_y.at[:, cols], y_held.at[i], sems.at[2 * i]),
                pltpu.make_async_copy(w_out.at[:, cols], w_held.at[i], sems.at[2 * i + 1]),
            )
        )
    for pair in copies:
        for copy in pair:
            copy.start()
    total = jnp.zeros(out.shape, f32)
    for i, pair in enumerate(copies):
        for copy in pair:
            copy.wait()
        total += lax.dot_general(y_held[i], w_held[i], NT, preferred_element_type=f32)
    out[...] = total.astype(bf16)


def forward_kernel(part, kb, bc, q_own, q_sib, kv, *refs):
    before = refs[0] if part else None
    out, qs, qt, acc, lst, sems = refs[part:]
    chip, core = my_chip(), lax.axis_index("core")
    copies = head_copies(qs, q_own, q_sib, sems)
    for copy in copies:
        copy.start()
    for copy in copies:
        copy.wait()

    def per_block(j, _):
        b = query_block(j, chip, core)
        qt[...] = qs[j].T
        acc[...] = before[j, :WIDTH, :] if part else jnp.zeros_like(acc)

        def visit(carry, idxs, limits):
            m, l, l_b = carry
            k = rows_of(kv, idxs)
            v = rows_of(kv, [i + 1 for i in idxs])
            s = jnp.dot(k, qt[...], preferred_element_type=f32) * (SCALE * LOG2E)
            if limits is not None:
                s = hide(s, limits, NEG)
            m_new = jnp.maximum(m, jnp.max(s, axis=0, keepdims=True))
            alpha = jnp.exp2(m - m_new)
            p = jnp.exp2(s - m_new)
            p_b = p.astype(bf16)
            o = lax.dot_general(v, p_b, TN, preferred_element_type=f32)
            acc[...] = acc[...] * alpha + o
            return (
                m_new,
                l * alpha + jnp.sum(p, axis=0, keepdims=True),
                l_b * alpha + jnp.sum(p_b.astype(f32), axis=0, keepdims=True),
            )

        zero = jnp.zeros((1, ROWS), f32)
        start = (jnp.full((1, ROWS), NEG, f32), zero, zero)
        if part:
            start = tuple(before[j, WIDTH + i : WIDTH + i + 1, :] for i in range(3))
        m, l, l_b = walk(kb, bc, lst, b, core, part, visit, start)
        out[j, :WIDTH, :] = acc[...]
        out[j, WIDTH : WIDTH + 8, :] = jnp.concatenate(
            [m, l, l_b, jnp.zeros((5, ROWS), f32)], axis=0
        )
        return 0

    lax.fori_loop(0, 4, per_block, 0)


def backward_kernel(
    part, kb, bc, q_own, q_sib, g_own, g_sib, kv_in, st_own, st_sib, *refs
):
    if part:
        dqt_in, dq_own, dq_sib, dkv, *scratch = refs
    else:
        dqt_out, dkv, *scratch = refs
    qs, gs, qt, gt, dq, kv, acc, held, lst, sems, out_sems = scratch
    chip, core = my_chip(), lax.axis_index("core")
    copies = [pltpu.make_async_copy(kv_in, kv, sems.at[4 * HEADS])]
    copies += head_copies(qs, q_own, q_sib, sems)
    for copy in copies:
        copy.start()
    stack_heads(gs, g_own, g_sib)
    acc[...] = jnp.zeros_like(acc)
    for copy in copies:
        copy.wait()

    def per_block(j, _):
        b = query_block(j, chip, core)
        peer = (j + 2) % 4
        qt[...] = qs[j].T
        gt[...] = gs[j].T
        m0, l0, n0 = (st_own[j, WIDTH + i : WIDTH + i + 1, :] for i in range(3))
        m1, l1, n1 = (st_sib[peer, WIDTH + i : WIDTH + i + 1, :] for i in range(3))
        m = jnp.maximum(m0, m1)
        a0, a1 = jnp.exp2(m0 - m), jnp.exp2(m1 - m)
        total = m + jnp.log(l0 * a0 + l1 * a1) * LOG2E
        o = st_own[j, :WIDTH, :] * a0 + st_sib[peer, :WIDTH, :] * a1
        delta = jnp.sum(o * gt[...].astype(f32), axis=0, keepdims=True) / (n0 * a0 + n1 * a1)
        dq[...] = dqt_in[j] if part else jnp.zeros_like(dq)

        def visit(carry, idxs, limits):
            k = rows_of(kv, idxs)
            v = rows_of(kv, [i + 1 for i in idxs])
            s = jnp.dot(k, qt[...], preferred_element_type=f32) * (SCALE * LOG2E)
            p = jnp.exp2(s - total)
            if limits is not None:
                p = hide(p, limits, 0.0)
            dp = jnp.dot(v, gt[...], preferred_element_type=f32)
            ds = (p * (dp - delta)).astype(bf16)
            dk = jnp.dot(ds, qs[j], preferred_element_type=f32)
            dv = jnp.dot(p.astype(bf16), gs[j], preferred_element_type=f32)
            for t, i in enumerate(idxs):
                acc[block_rows(i), :] += dk[t * SPAN : (t + 1) * SPAN]
                acc[block_rows(i + 1), :] += dv[t * SPAN : (t + 1) * SPAN]
            dq[...] += lax.dot_general(k, ds, TN, preferred_element_type=f32)
            return carry

        walk(kb, bc, lst, b, core, part, visit, 0)
        if not part:
            dqt_out[j] = dq[...]
            return 0
        row = pl.ds(pl.multiple_of((j % 2) * SPAN, SPAN), SPAN)
        for h in range(HEADS):
            piece = (dq[:, h * SPAN : (h + 1) * SPAN] * SCALE).astype(bf16).T

            @pl.when(j < 2)
            def _():
                dq_own[row, h * WIDTH : (h + 1) * WIDTH] = piece

            @pl.when(j >= 2)
            def _():
                dq_sib[row, h * WIDTH : (h + 1) * WIDTH] = piece

        return 0

    lax.fori_loop(0, 4, per_block, 0)
    half = SPAN
    copies = []
    for c in range(dkv.shape[0] // half):
        rows = slice(c * half, (c + 1) * half)
        at = 2 * c * half
        held[rows, :WIDTH] = (acc[at : at + half, :] * SCALE).astype(bf16)
        held[rows, WIDTH:] = acc[at + half : at + 2 * half, :].astype(bf16)
        copies.append(pltpu.make_async_copy(held.at[rows, :], dkv.at[rows, :], out_sems.at[c]))
        copies[-1].start()
    for copy in copies:
        copy.wait()


def per_device(queries, keys, values, d_y, w_out, key_blocks, block_count):
    chips = lax.axis_size("y") * lax.axis_size("x")
    tok = keys.shape[0]
    swap = [(0, 1), (1, 0)]
    smem = pl.BlockSpec(memory_space=pltpu.SMEM)
    vmem = pl.BlockSpec(memory_space=pltpu.VMEM)
    hbm = pl.BlockSpec(memory_space=pltpu.HBM)
    d_y_all = lax.all_gather(d_y, "head", axis=1, tiled=True)
    q_sib = lax.ppermute(queries, "core", swap)
    kv = []
    for part in range(2):
        kv_sent = pl.pallas_call(
            functools.partial(spread_kernel, part),
            out_shape=jax.ShapeDtypeStruct((chips, tok, WIDTH), bf16),
            in_specs=[vmem, vmem],
            out_specs=hbm,
            scratch_shapes=[pltpu.SemaphoreType.DMA((2 * chips,))],
            cost_estimate=pl.CostEstimate(
                flops=0, bytes_accessed=chips * tok * WIDTH * 2, transcendentals=0
            ),
            name="spread_keys_values",
        )(keys, values)
        if part:
            kv_sent, q_sib = lax.optimization_barrier((kv_sent, q_sib))
        kv.append(lax.all_to_all(kv_sent, CHIP_AXES, 0, 0).reshape(chips * tok, WIDTH))
    queries, q_sib = (pltpu.with_memory_space_constraint(q, pltpu.HBM) for q in (queries, q_sib))

    before = []
    for part in range(2):
        stats = pl.pallas_call(
            functools.partial(forward_kernel, part),
            out_shape=[pltpu.HBM, jax.ShapeDtypeStruct][part]((4, WIDTH + 8, ROWS), f32),
            in_specs=[smem, smem, hbm, hbm, vmem] + [vmem] * part,
            out_specs=vmem,
            scratch_shapes=[
                pltpu.VMEM((4, ROWS, WIDTH), bf16),
                pltpu.VMEM((WIDTH, ROWS), bf16),
                pltpu.VMEM((WIDTH, ROWS), f32),
                pltpu.SMEM((40,), jnp.int32),
                pltpu.SemaphoreType.DMA((4 * HEADS,)),
            ],
            compiler_params=pltpu.CompilerParams(vmem_limit_bytes=48 * 2**20),
            cost_estimate=pl.CostEstimate(
                flops=3 * 10**9, bytes_accessed=4 * 2**20, transcendentals=2 * 10**6
            ),
            name="forward_statistics",
        )(key_blocks, block_count, queries, q_sib, kv[part], *before)
        before = [pltpu.with_memory_space_constraint(stats, pltpu.HBM)]
    stats_sib = lax.ppermute(stats, "core", swap)

    att_grad = pl.pallas_call(
        project_kernel,
        out_shape=jax.ShapeDtypeStruct((tok, ROWS), bf16),
        in_specs=[hbm, hbm],
        out_specs=vmem,
        scratch_shapes=[
            pltpu.VMEM((PARTS, tok, w_out.shape[1] // PARTS), bf16),
            pltpu.VMEM((PARTS, w_out.shape[0], w_out.shape[1] // PARTS), bf16),
            pltpu.SemaphoreType.DMA((2 * PARTS,)),
        ],
        compiler_params=pltpu.CompilerParams(vmem_limit_bytes=32 * 2**20),
        cost_estimate=pl.CostEstimate(
            flops=2 * tok * w_out.size, bytes_accessed=6 * 2**20, transcendentals=0
        ),
        name="attention_cotangent",
    )(*(pltpu.with_memory_space_constraint(a, pltpu.HBM) for a in (d_y_all, w_out)))
    grad_sib = lax.ppermute(att_grad, "core", swap)

    partial_dq = []
    dkv = []
    for part in range(2):
        dq_shapes = [pltpu.HBM((4, WIDTH, ROWS), f32)]
        if part:
            dq_shapes = [jax.ShapeDtypeStruct((tok, ROWS), bf16)] * 2
        *partial_dq, sums = pl.pallas_call(
            functools.partial(backward_kernel, part),
            out_shape=(*dq_shapes, jax.ShapeDtypeStruct((chips * SPAN, 2 * WIDTH), bf16)),
            in_specs=[smem, smem, hbm, hbm, vmem, vmem, hbm, vmem, vmem] + [vmem] * part,
            out_specs=(*([vmem] * len(dq_shapes)), hbm),
            scratch_shapes=[
                pltpu.VMEM((4, ROWS, WIDTH), bf16),
                pltpu.VMEM((4, ROWS, WIDTH), bf16),
                pltpu.VMEM((WIDTH, ROWS), bf16),
                pltpu.VMEM((WIDTH, ROWS), bf16),
                pltpu.VMEM((WIDTH, ROWS), f32),
                pltpu.VMEM((chips * tok, WIDTH), bf16),
                pltpu.VMEM((chips * tok, WIDTH), f32),
                pltpu.VMEM((chips * SPAN, 2 * WIDTH), bf16),
                pltpu.SMEM((40,), jnp.int32),
                pltpu.SemaphoreType.DMA((4 * HEADS + 1,)),
                pltpu.SemaphoreType.DMA((chips,)),
            ],
            compiler_params=pltpu.CompilerParams(vmem_limit_bytes=48 * 2**20),
            cost_estimate=pl.CostEstimate(
                flops=5 * 10**9, bytes_accessed=6 * 2**20, transcendentals=2 * 10**6
            ),
            name="backward_gradients",
        )(
            key_blocks, block_count, queries, q_sib, att_grad, grad_sib, kv[part],
            stats, stats_sib,
            *(pltpu.with_memory_space_constraint(a, pltpu.HBM) for a in partial_dq),
        )
        parts = lax.all_to_all(sums.reshape(chips, SPAN, 2 * WIDTH), CHIP_AXES, 0, 0)
        dkv.append(jnp.sum(parts.astype(f32), axis=0).astype(bf16))

    dq_own, dq_sib = partial_dq
    d_queries = dq_own + lax.ppermute(dq_sib, "core", swap)
    summed = jnp.concatenate(dkv, axis=0)
    return d_queries, summed[:, :WIDTH], summed[:, WIDTH:]


def solution(mesh):
    ctx, head = mesh.devices.shape
    side = math.isqrt(ctx // 2)
    grid = Mesh(mesh.devices.reshape(side, side, 2, head), ("y", "x", "core", "head"))
    rows = P(TOKEN_AXES, "head")
    return jax.shard_map(
        per_device,
        mesh=grid,
        in_specs=(rows, rows, rows, rows, P("head", None), P(), P()),
        out_specs=(rows, rows, rows),
        check_vma=False,
    )
```

```python
import functools
import math

import jax
import jax.numpy as jnp
from jax import lax
from jax.experimental import pallas as pl
from jax.experimental.pallas import tpu as pltpu
from jax.sharding import Mesh
from jax.sharding import PartitionSpec as P

WIDTH = 128
SPAN = 128
HEADS = 4
ROWS = HEADS * SPAN
SCALE = 1.0 / math.sqrt(WIDTH)
LOG2E = 1.4426950408889634
NEG = -1e30
TILE = 4
PARTS = 4
CHIP_AXES = ("y", "x")
TOKEN_AXES = ("y", "x", "core")
NT = (((1,), (1,)), ((), ()))
TN = (((0,), (0,)), ((), ()))
f32 = jnp.float32
bf16 = jnp.bfloat16


def my_chip():
    return lax.axis_index("y") * lax.axis_size("x") + lax.axis_index("x")


def query_block(j, chip, core):
    side = jnp.where(j < 2, core, 1 - core)
    chips = lax.axis_size("y") * lax.axis_size("x")
    holder = jnp.where(side == 0, chip, chips - 1 - chip)
    return 4 * holder + 2 * side + j % 2


def head_block(j, h):
    return slice((j % 2) * SPAN, (j % 2 + 1) * SPAN), slice(h * WIDTH, (h + 1) * WIDTH)


def stack_heads(dst, own, sib):
    for j in range(4):
        src = own if j < 2 else sib
        for h in range(HEADS):
            dst[j, h * SPAN : (h + 1) * SPAN, :] = src[head_block(j, h)]


def head_copies(dst, own, sib, sems):
    copies = []
    for j in range(4):
        src = own if j < 2 else sib
        for h in range(HEADS):
            to = dst.at[j, h * SPAN : (h + 1) * SPAN, :]
            copies.append(
                pltpu.make_async_copy(src.at[head_block(j, h)], to, sems.at[j * HEADS + h])
            )
    return copies


def list_blocks(kb, bc, lst, b, core):
    def step(s, n):
        blk = kb[b, s]
        lst[n] = 4 * (blk // 4) + blk % 2
        return n + jnp.where((blk // 2) % 2 == core, 1, 0)

    n = lax.fori_loop(1, bc[b], step, 0)
    for t in range(TILE):
        lst[n + t] = 4 * (b // 4) + b % 2
    return n


def block_rows(i):
    return pl.ds(pl.multiple_of(i * SPAN, SPAN), SPAN)


def rows_of(ref, idxs):
    parts = [ref[block_rows(i), :] for i in idxs]
    return parts[0] if len(parts) == 1 else jnp.concatenate(parts, axis=0)


def hide(x, limits, fill):
    key = lax.broadcasted_iota(jnp.int32, (SPAN, ROWS), 0)
    qry = lax.broadcasted_iota(jnp.int32, (SPAN, ROWS), 1) % SPAN
    parts = [
        jnp.where(key - qry <= limit, x[t * SPAN : (t + 1) * SPAN], fill)
        for t, limit in enumerate(limits)
    ]
    return jnp.concatenate(parts, axis=0)


def walk(kb, bc, lst, b, core, visit, carry):
    n = list_blocks(kb, bc, lst, b, core)
    has_diag = jnp.where((b // 2) % 2 == core, 1, 0)
    tiles = n // TILE
    done = tiles * TILE
    rest = n - done
    left = rest + has_diag
    carry = lax.fori_loop(
        0, tiles, lambda t, c: visit(c, [lst[t * TILE + i] for i in range(TILE)], None), carry
    )

    def last(count):
        def run(c):
            limits = [
                jnp.where(t < rest, SPAN, jnp.where(t == rest, has_diag * 2 * SPAN, 0) - 2 * SPAN)
                for t in range(count)
            ]
            return visit(c, [lst[done + t] for t in range(count)], limits)

        return run

    def some(c):
        return lax.cond(left <= TILE // 2, last(TILE // 2), last(TILE), c)

    return lax.cond(left > 0, some, lambda c: c, carry)


def spread_kernel(keys, values, out, sems):
    chips, tok = out.shape[0], keys.shape[0]
    copies = []
    for c in range(chips):
        copies.append(pltpu.make_async_copy(keys, out.at[c, :tok, :], sems.at[2 * c]))
        copies.append(pltpu.make_async_copy(values, out.at[c, tok:, :], sems.at[2 * c + 1]))
    for copy in copies:
        copy.start()
    for copy in copies:
        copy.wait()


def project_kernel(d_y, w_out, out, y_held, w_held, sems):
    width = y_held.shape[2]
    copies = []
    for i in range(PARTS):
        cols = slice(i * width, (i + 1) * width)
        copies.append(
            (
                pltpu.make_async_copy(d_y.at[:, cols], y_held.at[i], sems.at[2 * i]),
                pltpu.make_async_copy(w_out.at[:, cols], w_held.at[i], sems.at[2 * i + 1]),
            )
        )
    for pair in copies:
        for copy in pair:
            copy.start()
    total = jnp.zeros(out.shape, f32)
    for i, pair in enumerate(copies):
        for copy in pair:
            copy.wait()
        total += lax.dot_general(y_held[i], w_held[i], NT, preferred_element_type=f32)
    out[...] = total.astype(bf16)


def forward_kernel(kb, bc, q_own, q_sib, kv, out, qs, qt, acc, lst, sems):
    chip, core = my_chip(), lax.axis_index("core")
    copies = head_copies(qs, q_own, q_sib, sems)
    for copy in copies:
        copy.start()
    for copy in copies:
        copy.wait()

    def per_block(j, _):
        b = query_block(j, chip, core)
        qt[...] = qs[j].T
        acc[...] = jnp.zeros_like(acc)

        def visit(carry, idxs, limits):
            m, l, l_b = carry
            k = rows_of(kv, idxs)
            v = rows_of(kv, [i + 2 for i in idxs])
            s = jnp.dot(k, qt[...], preferred_element_type=f32) * (SCALE * LOG2E)
            if limits is not None:
                s = hide(s, limits, NEG)
            m_new = jnp.maximum(m, jnp.max(s, axis=0, keepdims=True))
            alpha = jnp.exp2(m - m_new)
            p = jnp.exp2(s - m_new)
            p_b = p.astype(bf16)
            o = lax.dot_general(v, p_b, TN, preferred_element_type=f32)
            acc[...] = acc[...] * alpha + o
            return (
                m_new,
                l * alpha + jnp.sum(p, axis=0, keepdims=True),
                l_b * alpha + jnp.sum(p_b.astype(f32), axis=0, keepdims=True),
            )

        zero = jnp.zeros((1, ROWS), f32)
        m, l, l_b = walk(
            kb, bc, lst, b, core, visit, (jnp.full((1, ROWS), NEG, f32), zero, zero)
        )
        out[j, :WIDTH, :] = acc[...]
        out[j, WIDTH : WIDTH + 8, :] = jnp.concatenate(
            [m, l, l_b, jnp.zeros((5, ROWS), f32)], axis=0
        )
        return 0

    lax.fori_loop(0, 4, per_block, 0)


def backward_kernel(
    kb, bc, q_own, q_sib, g_own, g_sib, kv_in, st_own, st_sib,
    dq_own, dq_sib, dkv,
    qs, gs, qt, gt, dq, kv, acc, held, lst, sems, out_sems,
):
    chip, core = my_chip(), lax.axis_index("core")
    copies = [pltpu.make_async_copy(kv_in, kv, sems.at[4 * HEADS])]
    copies += head_copies(qs, q_own, q_sib, sems)
    for copy in copies:
        copy.start()
    stack_heads(gs, g_own, g_sib)
    acc[...] = jnp.zeros_like(acc)
    for copy in copies:
        copy.wait()

    def per_block(j, _):
        b = query_block(j, chip, core)
        peer = (j + 2) % 4
        qt[...] = qs[j].T
        gt[...] = gs[j].T
        m0, l0, n0 = (st_own[j, WIDTH + i : WIDTH + i + 1, :] for i in range(3))
        m1, l1, n1 = (st_sib[peer, WIDTH + i : WIDTH + i + 1, :] for i in range(3))
        m = jnp.maximum(m0, m1)
        a0, a1 = jnp.exp2(m0 - m), jnp.exp2(m1 - m)
        total = m + jnp.log(l0 * a0 + l1 * a1) * LOG2E
        o = st_own[j, :WIDTH, :] * a0 + st_sib[peer, :WIDTH, :] * a1
        delta = jnp.sum(o * gt[...].astype(f32), axis=0, keepdims=True) / (n0 * a0 + n1 * a1)
        dq[...] = jnp.zeros_like(dq)

        def visit(carry, idxs, limits):
            k = rows_of(kv, idxs)
            v = rows_of(kv, [i + 2 for i in idxs])
            s = jnp.dot(k, qt[...], preferred_element_type=f32) * (SCALE * LOG2E)
            p = jnp.exp2(s - total)
            if limits is not None:
                p = hide(p, limits, 0.0)
            dp = jnp.dot(v, gt[...], preferred_element_type=f32)
            ds = (p * (dp - delta)).astype(bf16)
            dk = jnp.dot(ds, qs[j], preferred_element_type=f32)
            dv = jnp.dot(p.astype(bf16), gs[j], preferred_element_type=f32)
            for t, i in enumerate(idxs):
                acc[block_rows(i), :] += dk[t * SPAN : (t + 1) * SPAN]
                acc[block_rows(i + 2), :] += dv[t * SPAN : (t + 1) * SPAN]
            dq[...] += lax.dot_general(k, ds, TN, preferred_element_type=f32)
            return carry

        walk(kb, bc, lst, b, core, visit, 0)
        row = pl.ds(pl.multiple_of((j % 2) * SPAN, SPAN), SPAN)
        for h in range(HEADS):
            piece = (dq[:, h * SPAN : (h + 1) * SPAN] * SCALE).astype(bf16).T

            @pl.when(j < 2)
            def _():
                dq_own[row, h * WIDTH : (h + 1) * WIDTH] = piece

            @pl.when(j >= 2)
            def _():
                dq_sib[row, h * WIDTH : (h + 1) * WIDTH] = piece

        return 0

    lax.fori_loop(0, 4, per_block, 0)
    half = 2 * SPAN
    copies = []
    for c in range(dkv.shape[0] // half):
        rows = slice(c * half, (c + 1) * half)
        at = 2 * c * half
        held[rows, :WIDTH] = (acc[at : at + half, :] * SCALE).astype(bf16)
        held[rows, WIDTH:] = acc[at + half : at + 2 * half, :].astype(bf16)
        copies.append(pltpu.make_async_copy(held.at[rows, :], dkv.at[rows, :], out_sems.at[c]))
        copies[-1].start()
    for copy in copies:
        copy.wait()


def per_device(queries, keys, values, d_y, w_out, key_blocks, block_count):
    chips = lax.axis_size("y") * lax.axis_size("x")
    tok = keys.shape[0]
    swap = [(0, 1), (1, 0)]
    smem = pl.BlockSpec(memory_space=pltpu.SMEM)
    vmem = pl.BlockSpec(memory_space=pltpu.VMEM)
    hbm = pl.BlockSpec(memory_space=pltpu.HBM)
    fold = [
        (2 * i + c, 2 * i if c == 0 else 2 * (chips - 1 - i) + 1)
        for i in range(chips)
        for c in range(2)
    ]
    d_y = lax.ppermute(d_y, TOKEN_AXES, fold)
    kv_sent = pl.pallas_call(
        spread_kernel,
        out_shape=jax.ShapeDtypeStruct((chips, 2 * tok, WIDTH), bf16),
        in_specs=[vmem, vmem],
        out_specs=hbm,
        scratch_shapes=[pltpu.SemaphoreType.DMA((2 * chips,))],
        cost_estimate=pl.CostEstimate(
            flops=0, bytes_accessed=chips * 2 * tok * WIDTH * 2, transcendentals=0
        ),
        name="spread_keys_values",
    )(keys, values)
    d_y, kv_sent = lax.optimization_barrier((d_y, kv_sent))
    d_y_all = lax.all_gather(d_y, "head", axis=1, tiled=True)
    kv = lax.all_to_all(kv_sent, CHIP_AXES, 0, 0).reshape(chips * 2 * tok, WIDTH)
    queries = lax.ppermute(queries, TOKEN_AXES, fold)
    q_sib = lax.ppermute(queries, "core", swap)
    queries, q_sib = (pltpu.with_memory_space_constraint(q, pltpu.HBM) for q in (queries, q_sib))

    stats = pl.pallas_call(
        forward_kernel,
        out_shape=jax.ShapeDtypeStruct((4, WIDTH + 8, ROWS), f32),
        in_specs=[smem, smem, hbm, hbm, vmem],
        out_specs=vmem,
        scratch_shapes=[
            pltpu.VMEM((4, ROWS, WIDTH), bf16),
            pltpu.VMEM((WIDTH, ROWS), bf16),
            pltpu.VMEM((WIDTH, ROWS), f32),
            pltpu.SMEM((40,), jnp.int32),
            pltpu.SemaphoreType.DMA((4 * HEADS,)),
        ],
        compiler_params=pltpu.CompilerParams(vmem_limit_bytes=48 * 2**20),
        cost_estimate=pl.CostEstimate(
            flops=6 * 10**9, bytes_accessed=4 * 2**20, transcendentals=4 * 10**6
        ),
        name="forward_statistics",
    )(key_blocks, block_count, queries, q_sib, kv)
    stats_sib = lax.ppermute(stats, "core", swap)

    att_grad = pl.pallas_call(
        project_kernel,
        out_shape=jax.ShapeDtypeStruct((tok, ROWS), bf16),
        in_specs=[hbm, hbm],
        out_specs=vmem,
        scratch_shapes=[
            pltpu.VMEM((PARTS, tok, w_out.shape[1] // PARTS), bf16),
            pltpu.VMEM((PARTS, w_out.shape[0], w_out.shape[1] // PARTS), bf16),
            pltpu.SemaphoreType.DMA((2 * PARTS,)),
        ],
        compiler_params=pltpu.CompilerParams(vmem_limit_bytes=32 * 2**20),
        cost_estimate=pl.CostEstimate(
            flops=2 * tok * w_out.size, bytes_accessed=6 * 2**20, transcendentals=0
        ),
        name="attention_cotangent",
    )(*(pltpu.with_memory_space_constraint(a, pltpu.HBM) for a in (d_y_all, w_out)))
    grad_sib = lax.ppermute(att_grad, "core", swap)

    dq_own, dq_sib, dkv = pl.pallas_call(
        backward_kernel,
        out_shape=(
            jax.ShapeDtypeStruct((tok, ROWS), bf16),
            jax.ShapeDtypeStruct((tok, ROWS), bf16),
            jax.ShapeDtypeStruct((chips * tok, 2 * WIDTH), bf16),
        ),
        in_specs=[smem, smem, hbm, hbm, vmem, vmem, hbm, vmem, vmem],
        out_specs=(vmem, vmem, hbm),
        scratch_shapes=[
            pltpu.VMEM((4, ROWS, WIDTH), bf16),
            pltpu.VMEM((4, ROWS, WIDTH), bf16),
            pltpu.VMEM((WIDTH, ROWS), bf16),
            pltpu.VMEM((WIDTH, ROWS), bf16),
            pltpu.VMEM((WIDTH, ROWS), f32),
            pltpu.VMEM((chips * 2 * tok, WIDTH), bf16),
            pltpu.VMEM((chips * 2 * tok, WIDTH), f32),
            pltpu.VMEM((chips * tok, 2 * WIDTH), bf16),
            pltpu.SMEM((40,), jnp.int32),
            pltpu.SemaphoreType.DMA((4 * HEADS + 1,)),
            pltpu.SemaphoreType.DMA((chips,)),
        ],
        compiler_params=pltpu.CompilerParams(vmem_limit_bytes=48 * 2**20),
        cost_estimate=pl.CostEstimate(
            flops=10 * 10**9, bytes_accessed=8 * 2**20, transcendentals=4 * 10**6
        ),
        name="backward_gradients",
    )(key_blocks, block_count, queries, q_sib, att_grad, grad_sib, kv, stats, stats_sib)

    d_queries = lax.ppermute(dq_own + lax.ppermute(dq_sib, "core", swap), TOKEN_AXES, fold)
    parts = lax.all_to_all(dkv.reshape(chips, tok, 2 * WIDTH), CHIP_AXES, 0, 0)
    summed = jnp.sum(parts.astype(f32), axis=0).astype(bf16)
    return d_queries, summed[:, :WIDTH], summed[:, WIDTH:]


def solution(mesh):
    ctx, head = mesh.devices.shape
    side = math.isqrt(ctx // 2)
    grid = Mesh(mesh.devices.reshape(side, side, 2, head), ("y", "x", "core", "head"))
    rows = P(TOKEN_AXES, "head")
    return jax.shard_map(
        per_device,
        mesh=grid,
        in_specs=(rows, rows, rows, rows, P("head", None), P(), P()),
        out_specs=(rows, rows, rows),
        check_vma=False,
    )
```

```python
import functools
import math

import jax
import jax.numpy as jnp
from jax import lax
from jax.experimental import pallas as pl
from jax.experimental.pallas import tpu as pltpu
from jax.sharding import Mesh
from jax.sharding import PartitionSpec as P

WIDTH = 128
SPAN = 128
HEADS = 4
ROWS = HEADS * SPAN
SCALE = 1.0 / math.sqrt(WIDTH)
LOG2E = 1.4426950408889634
NEG = -1e30
TILE = 4
PARTS = 4
CHIP_AXES = ("y", "x")
TOKEN_AXES = ("y", "x", "core")
NT = (((1,), (1,)), ((), ()))
TN = (((0,), (0,)), ((), ()))
f32 = jnp.float32
bf16 = jnp.bfloat16


def my_chip():
    return lax.axis_index("y") * lax.axis_size("x") + lax.axis_index("x")


def query_block(j, chip, core):
    side = jnp.where(j < 2, core, 1 - core)
    chips = lax.axis_size("y") * lax.axis_size("x")
    holder = jnp.where(side == 0, chip, chips - 1 - chip)
    return 4 * holder + 2 * side + j % 2


def head_block(j, h):
    return slice((j % 2) * SPAN, (j % 2 + 1) * SPAN), slice(h * WIDTH, (h + 1) * WIDTH)


def stack_heads(dst, own, sib):
    for j in range(4):
        src = own if j < 2 else sib
        for h in range(HEADS):
            dst[j, h * SPAN : (h + 1) * SPAN, :] = src[head_block(j, h)]


def head_copies(dst, own, sib, sems):
    copies = []
    for j in range(4):
        src = own if j < 2 else sib
        for h in range(HEADS):
            to = dst.at[j, h * SPAN : (h + 1) * SPAN, :]
            copies.append(
                pltpu.make_async_copy(src.at[head_block(j, h)], to, sems.at[j * HEADS + h])
            )
    return copies


def list_blocks(kb, bc, lst, b, core):
    def step(s, n):
        blk = kb[b, s]
        lst[n] = 4 * (blk // 4) + blk % 2
        return n + jnp.where((blk // 2) % 2 == core, 1, 0)

    n = lax.fori_loop(1, bc[b], step, 0)
    for t in range(TILE):
        lst[n + t] = 4 * (b // 4) + b % 2
    return n


def block_rows(i):
    return pl.ds(pl.multiple_of(i * SPAN, SPAN), SPAN)


def rows_of(ref, idxs):
    parts = [ref[block_rows(i), :] for i in idxs]
    return parts[0] if len(parts) == 1 else jnp.concatenate(parts, axis=0)


def hide(x, limits, fill):
    key = lax.broadcasted_iota(jnp.int32, (SPAN, ROWS), 0)
    qry = lax.broadcasted_iota(jnp.int32, (SPAN, ROWS), 1) % SPAN
    parts = [
        jnp.where(key - qry <= limit, x[t * SPAN : (t + 1) * SPAN], fill)
        for t, limit in enumerate(limits)
    ]
    return jnp.concatenate(parts, axis=0)


def walk(kb, bc, lst, b, core, visit, carry):
    n = list_blocks(kb, bc, lst, b, core)
    has_diag = jnp.where((b // 2) % 2 == core, 1, 0)
    tiles = n // TILE
    done = tiles * TILE
    rest = n - done
    left = rest + has_diag
    carry = lax.fori_loop(
        0, tiles, lambda t, c: visit(c, [lst[t * TILE + i] for i in range(TILE)], None), carry
    )

    def last(count):
        def run(c):
            limits = [
                jnp.where(t < rest, SPAN, jnp.where(t == rest, has_diag * 2 * SPAN, 0) - 2 * SPAN)
                for t in range(count)
            ]
            return visit(c, [lst[done + t] for t in range(count)], limits)

        return run

    def some(c):
        return lax.cond(left <= TILE // 2, last(TILE // 2), last(TILE), c)

    return lax.cond(left > 0, some, lambda c: c, carry)


def spread_kernel(keys, values, out, sems):
    chips, tok = out.shape[0], keys.shape[0]
    copies = []
    for c in range(chips):
        copies.append(pltpu.make_async_copy(keys, out.at[c, :tok, :], sems.at[2 * c]))
        copies.append(pltpu.make_async_copy(values, out.at[c, tok:, :], sems.at[2 * c + 1]))
    for copy in copies:
        copy.start()
    for copy in copies:
        copy.wait()


def project_kernel(d_y, w_out, out, y_held, w_held, sems):
    width = y_held.shape[2]
    copies = []
    for i in range(PARTS):
        cols = slice(i * width, (i + 1) * width)
        copies.append(
            (
                pltpu.make_async_copy(d_y.at[:, cols], y_held.at[i], sems.at[2 * i]),
                pltpu.make_async_copy(w_out.at[:, cols], w_held.at[i], sems.at[2 * i + 1]),
            )
        )
    for pair in copies:
        for copy in pair:
            copy.start()
    total = jnp.zeros(out.shape, f32)
    for i, pair in enumerate(copies):
        for copy in pair:
            copy.wait()
        total += lax.dot_general(y_held[i], w_held[i], NT, preferred_element_type=f32)
    out[...] = total.astype(bf16)


def forward_kernel(kb, bc, q_own, q_sib, kv, out, qs, qt, acc, lst, sems):
    chip, core = my_chip(), lax.axis_index("core")
    copies = head_copies(qs, q_own, q_sib, sems)
    for copy in copies:
        copy.start()
    for copy in copies:
        copy.wait()

    def per_block(j, _):
        b = query_block(j, chip, core)
        qt[...] = qs[j].T
        acc[...] = jnp.zeros_like(acc)

        def visit(carry, idxs, limits):
            m, l, l_b = carry
            k = rows_of(kv, idxs)
            v = rows_of(kv, [i + 2 for i in idxs])
            s = jnp.dot(k, qt[...], preferred_element_type=f32) * (SCALE * LOG2E)
            if limits is not None:
                s = hide(s, limits, NEG)
            m_new = jnp.maximum(m, jnp.max(s, axis=0, keepdims=True))
            alpha = jnp.exp2(m - m_new)
            p = jnp.exp2(s - m_new)
            p_b = p.astype(bf16)
            o = lax.dot_general(v, p_b, TN, preferred_element_type=f32)
            acc[...] = acc[...] * alpha + o
            return (
                m_new,
                l * alpha + jnp.sum(p, axis=0, keepdims=True),
                l_b * alpha + jnp.sum(p_b.astype(f32), axis=0, keepdims=True),
            )

        zero = jnp.zeros((1, ROWS), f32)
        m, l, l_b = walk(
            kb, bc, lst, b, core, visit, (jnp.full((1, ROWS), NEG, f32), zero, zero)
        )
        out[j, :WIDTH, :] = acc[...]
        out[j, WIDTH : WIDTH + 8, :] = jnp.concatenate(
            [m, l, l_b, jnp.zeros((5, ROWS), f32)], axis=0
        )
        return 0

    lax.fori_loop(0, 4, per_block, 0)


def backward_kernel(
    kb, bc, q_own, q_sib, g_own, g_sib, kv_in, st_own, st_sib,
    dq_own, dq_sib, dkv,
    qs, gs, qt, gt, dq, kv, acc, held, lst, sems, out_sems,
):
    chip, core = my_chip(), lax.axis_index("core")
    copies = [pltpu.make_async_copy(kv_in, kv, sems.at[4 * HEADS])]
    copies += head_copies(qs, q_own, q_sib, sems)
    for copy in copies:
        copy.start()
    stack_heads(gs, g_own, g_sib)
    acc[...] = jnp.zeros_like(acc)
    for copy in copies:
        copy.wait()

    def per_block(j, _):
        b = query_block(j, chip, core)
        peer = (j + 2) % 4
        qt[...] = qs[j].T
        gt[...] = gs[j].T
        m0, l0, n0 = (st_own[j, WIDTH + i : WIDTH + i + 1, :] for i in range(3))
        m1, l1, n1 = (st_sib[peer, WIDTH + i : WIDTH + i + 1, :] for i in range(3))
        m = jnp.maximum(m0, m1)
        a0, a1 = jnp.exp2(m0 - m), jnp.exp2(m1 - m)
        total = m + jnp.log(l0 * a0 + l1 * a1) * LOG2E
        o = st_own[j, :WIDTH, :] * a0 + st_sib[peer, :WIDTH, :] * a1
        delta = jnp.sum(o * gt[...].astype(f32), axis=0, keepdims=True) / (n0 * a0 + n1 * a1)
        dq[...] = jnp.zeros_like(dq)

        def visit(carry, idxs, limits):
            k = rows_of(kv, idxs)
            v = rows_of(kv, [i + 2 for i in idxs])
            s = jnp.dot(k, qt[...], preferred_element_type=f32) * (SCALE * LOG2E)
            p = jnp.exp2(s - total)
            if limits is not None:
                p = hide(p, limits, 0.0)
            dp = jnp.dot(v, gt[...], preferred_element_type=f32)
            ds = (p * (dp - delta)).astype(bf16)
            dk = jnp.dot(ds, qs[j], preferred_element_type=f32)
            dv = jnp.dot(p.astype(bf16), gs[j], preferred_element_type=f32)
            for t, i in enumerate(idxs):
                acc[block_rows(i), :] += dk[t * SPAN : (t + 1) * SPAN]
                acc[block_rows(i + 2), :] += dv[t * SPAN : (t + 1) * SPAN]
            dq[...] += lax.dot_general(k, ds, TN, preferred_element_type=f32)
            return carry

        walk(kb, bc, lst, b, core, visit, 0)
        row = pl.ds(pl.multiple_of((j % 2) * SPAN, SPAN), SPAN)
        for h in range(HEADS):
            piece = (dq[:, h * SPAN : (h + 1) * SPAN] * SCALE).astype(bf16).T

            @pl.when(j < 2)
            def _():
                dq_own[row, h * WIDTH : (h + 1) * WIDTH] = piece

            @pl.when(j >= 2)
            def _():
                dq_sib[row, h * WIDTH : (h + 1) * WIDTH] = piece

        return 0

    lax.fori_loop(0, 4, per_block, 0)
    half = 2 * SPAN
    copies = []
    for c in range(dkv.shape[0] // half):
        rows = slice(c * half, (c + 1) * half)
        at = 2 * c * half
        held[rows, :WIDTH] = (acc[at : at + half, :] * SCALE).astype(bf16)
        held[rows, WIDTH:] = acc[at + half : at + 2 * half, :].astype(bf16)
        copies.append(pltpu.make_async_copy(held.at[rows, :], dkv.at[rows, :], out_sems.at[c]))
        copies[-1].start()
    for copy in copies:
        copy.wait()


def finish_kernel(parts, dq, dq_out, keys_out, values_out, sem):
    copy = pltpu.make_async_copy(dq, dq_out, sem)
    copy.start()
    rows = 64
    for r in range(0, keys_out.shape[0], rows):
        at = slice(r, r + rows)
        total = parts[0, at, :].astype(f32)
        for c in range(1, parts.shape[0]):
            total += parts[c, at, :].astype(f32)
        keys_out[at, :] = total[:, :WIDTH].astype(bf16)
        values_out[at, :] = total[:, WIDTH:].astype(bf16)
    copy.wait()


def per_device(queries, keys, values, d_y, w_out, key_blocks, block_count):
    chips = lax.axis_size("y") * lax.axis_size("x")
    tok = keys.shape[0]
    swap = [(0, 1), (1, 0)]
    smem = pl.BlockSpec(memory_space=pltpu.SMEM)
    vmem = pl.BlockSpec(memory_space=pltpu.VMEM)
    hbm = pl.BlockSpec(memory_space=pltpu.HBM)
    fold = [
        (2 * i + c, 2 * i if c == 0 else 2 * (chips - 1 - i) + 1)
        for i in range(chips)
        for c in range(2)
    ]
    d_y = lax.ppermute(d_y, TOKEN_AXES, fold)
    kv_sent = pl.pallas_call(
        spread_kernel,
        out_shape=jax.ShapeDtypeStruct((chips, 2 * tok, WIDTH), bf16),
        in_specs=[vmem, vmem],
        out_specs=hbm,
        scratch_shapes=[pltpu.SemaphoreType.DMA((2 * chips,))],
        cost_estimate=pl.CostEstimate(
            flops=0, bytes_accessed=chips * 2 * tok * WIDTH * 2, transcendentals=0
        ),
        name="spread_keys_values",
    )(keys, values)
    d_y, kv_sent = lax.optimization_barrier((d_y, kv_sent))
    d_y_all = lax.all_gather(d_y, "head", axis=1, tiled=True)
    kv = lax.all_to_all(kv_sent, CHIP_AXES, 0, 0).reshape(chips * 2 * tok, WIDTH)
    queries = lax.ppermute(queries, TOKEN_AXES, fold)
    q_sib = lax.ppermute(queries, "core", swap)
    queries, q_sib = (pltpu.with_memory_space_constraint(q, pltpu.HBM) for q in (queries, q_sib))

    stats = pl.pallas_call(
        forward_kernel,
        out_shape=jax.ShapeDtypeStruct((4, WIDTH + 8, ROWS), f32),
        in_specs=[smem, smem, hbm, hbm, vmem],
        out_specs=vmem,
        scratch_shapes=[
            pltpu.VMEM((4, ROWS, WIDTH), bf16),
            pltpu.VMEM((WIDTH, ROWS), bf16),
            pltpu.VMEM((WIDTH, ROWS), f32),
            pltpu.SMEM((40,), jnp.int32),
            pltpu.SemaphoreType.DMA((4 * HEADS,)),
        ],
        compiler_params=pltpu.CompilerParams(vmem_limit_bytes=48 * 2**20),
        cost_estimate=pl.CostEstimate(
            flops=6 * 10**9, bytes_accessed=4 * 2**20, transcendentals=4 * 10**6
        ),
        name="forward_statistics",
    )(key_blocks, block_count, queries, q_sib, kv)
    stats_sib = lax.ppermute(stats, "core", swap)

    att_grad = pl.pallas_call(
        project_kernel,
        out_shape=jax.ShapeDtypeStruct((tok, ROWS), bf16),
        in_specs=[hbm, hbm],
        out_specs=vmem,
        scratch_shapes=[
            pltpu.VMEM((PARTS, tok, w_out.shape[1] // PARTS), bf16),
            pltpu.VMEM((PARTS, w_out.shape[0], w_out.shape[1] // PARTS), bf16),
            pltpu.SemaphoreType.DMA((2 * PARTS,)),
        ],
        compiler_params=pltpu.CompilerParams(vmem_limit_bytes=32 * 2**20),
        cost_estimate=pl.CostEstimate(
            flops=2 * tok * w_out.size, bytes_accessed=6 * 2**20, transcendentals=0
        ),
        name="attention_cotangent",
    )(*(pltpu.with_memory_space_constraint(a, pltpu.HBM) for a in (d_y_all, w_out)))
    grad_sib = lax.ppermute(att_grad, "core", swap)

    dq_own, dq_sib, dkv = pl.pallas_call(
        backward_kernel,
        out_shape=(
            jax.ShapeDtypeStruct((tok, ROWS), bf16),
            jax.ShapeDtypeStruct((tok, ROWS), bf16),
            jax.ShapeDtypeStruct((chips * tok, 2 * WIDTH), bf16),
        ),
        in_specs=[smem, smem, hbm, hbm, vmem, vmem, hbm, vmem, vmem],
        out_specs=(vmem, vmem, hbm),
        scratch_shapes=[
            pltpu.VMEM((4, ROWS, WIDTH), bf16),
            pltpu.VMEM((4, ROWS, WIDTH), bf16),
            pltpu.VMEM((WIDTH, ROWS), bf16),
            pltpu.VMEM((WIDTH, ROWS), bf16),
            pltpu.VMEM((WIDTH, ROWS), f32),
            pltpu.VMEM((chips * 2 * tok, WIDTH), bf16),
            pltpu.VMEM((chips * 2 * tok, WIDTH), f32),
            pltpu.VMEM((chips * tok, 2 * WIDTH), bf16),
            pltpu.SMEM((40,), jnp.int32),
            pltpu.SemaphoreType.DMA((4 * HEADS + 1,)),
            pltpu.SemaphoreType.DMA((chips,)),
        ],
        compiler_params=pltpu.CompilerParams(vmem_limit_bytes=48 * 2**20),
        cost_estimate=pl.CostEstimate(
            flops=10 * 10**9, bytes_accessed=8 * 2**20, transcendentals=4 * 10**6
        ),
        name="backward_gradients",
    )(key_blocks, block_count, queries, q_sib, att_grad, grad_sib, kv, stats, stats_sib)

    d_queries = lax.ppermute(dq_own + lax.ppermute(dq_sib, "core", swap), TOKEN_AXES, fold)
    parts = lax.all_to_all(dkv.reshape(chips, tok, 2 * WIDTH), CHIP_AXES, 0, 0)
    return pl.pallas_call(
        finish_kernel,
        out_shape=(
            jax.ShapeDtypeStruct((tok, ROWS), bf16),
            jax.ShapeDtypeStruct((tok, WIDTH), bf16),
            jax.ShapeDtypeStruct((tok, WIDTH), bf16),
        ),
        in_specs=[vmem, vmem],
        out_specs=(hbm, vmem, vmem),
        scratch_shapes=[pltpu.SemaphoreType.DMA(())],
        compiler_params=pltpu.CompilerParams(vmem_limit_bytes=16 * 2**20),
        cost_estimate=pl.CostEstimate(
            flops=chips * tok * 2 * WIDTH, bytes_accessed=3 * 2**20, transcendentals=0
        ),
        name="sum_partial_gradients",
    )(parts, d_queries)


def solution(mesh):
    ctx, head = mesh.devices.shape
    side = math.isqrt(ctx // 2)
    grid = Mesh(mesh.devices.reshape(side, side, 2, head), ("y", "x", "core", "head"))
    rows = P(TOKEN_AXES, "head")
    return jax.shard_map(
        per_device,
        mesh=grid,
        in_specs=(rows, rows, rows, rows, P("head", None), P(), P()),
        out_specs=(rows, rows, rows),
        check_vma=False,
    )
```
